512 devices in a mesh: sector: 256 (over y, z, x_lo, core), radial: 2 (over x_hi).
Axes of the slice: x: 4 (x_hi: 2, x_lo: 2; x = x_hi * 2 + x_lo), y: 4, z: 16, core: 2. Of those that a mesh axis runs over, the one named last changes fastest.
Arguments:
- positions: float32 [8192, 512], P(('sector', 'radial')), may hold values from -6 to 6
- stiffness: float32 [8192], P(('sector', 'radial')), may hold values from 1 to 100
- blocks: bfloat16 [2, 1536, 512, 512], P(None, ('sector', 'radial')), may hold values from -0.0625 to 0.0625
- pair_src: int32 [2, 1536], P(None, ('sector', 'radial')), may hold values from 0 to 8191, as said below
- pair_tgt: int32 [2, 1536], P(None, ('sector', 'radial')), may hold values from 0 to 8191, as said below
- cross_slots: int32 [512, 1], P(('sector', 'radial')), may hold values from 0 to 15, as said below
Outputs:
- after_crossing: float32 [8192, 512], P(('sector', 'radial'))
- final_positions: float32 [8192, 512], P(('sector', 'radial'))
The draws below stay inside these ranges and needn't reach their ends.
Inputs may be any that keep to these rules, and one draw needn't show every extreme that they name: `pair_src`: the pair at position p has its source among the 16 vesicles of the device that holds position p, that is from p // 3 * 16 on. `pair_tgt`: of the 3 pairs that a device holds, the first 1 target vesicles of the previous sector around the loop, the next 1 vesicles of its own sector, the last 1 vesicles of the next sector, in either radial sub-band. `cross_slots`: the 1 slots of a row are different.
All inputs are finite; a program needn't handle non-finite values.
Results may differ from the reference program's by a relative error of at most 0.0003.
Values may be sent and summed in bfloat16 or wider, within the bound.
A program may use at most 64 MiB of HBM per device.

```python
import math
import jax
import jax.numpy as jnp
from jax import lax

P_SIZE = 256
VES_DEV = 16
PAIR_OFF = 1
CROSS = 1
ITERS = 3
STEPS = 2
VESICLES = 8192
PAIRS = 1536
N_SECTOR = 256
N_RADIAL = 2


def draw_pair_src(key, part):
    position = jnp.arange(PAIRS, dtype=jnp.int32)
    owner = position // (3 * PAIR_OFF)
    slot = jax.random.randint(key, (STEPS, PAIRS), 0, VES_DEV, dtype=jnp.int32)
    slot = slot.at[0, 0].set(0)
    slot = slot.at[STEPS - 1, PAIRS - 1].set(VES_DEV - 1)
    return (owner[None, :] * VES_DEV + slot).astype(jnp.int32)


def draw_pair_tgt(key, part):
    position = jnp.arange(PAIRS, dtype=jnp.int32)
    owner = position // (3 * PAIR_OFF)
    sector_own = owner // N_RADIAL
    offset = position % (3 * PAIR_OFF) // PAIR_OFF - 1
    target_sector = (sector_own + offset) % N_SECTOR
    key_radial = jax.random.fold_in(key, 11)
    key_slot = jax.random.fold_in(key, 23)
    target_radial = jax.random.randint(key_radial, (STEPS, PAIRS), 0, N_RADIAL, dtype=jnp.int32)
    target_slot = jax.random.randint(key_slot, (STEPS, PAIRS), 0, VES_DEV, dtype=jnp.int32)
    chosen = (target_sector[None, :] * N_RADIAL + target_radial) * VES_DEV + target_slot
    chosen = chosen.at[0, PAIR_OFF].set(0)
    last_group = (N_SECTOR * N_RADIAL - 1) * 3 * PAIR_OFF + PAIR_OFF
    chosen = chosen.at[0, last_group].set(VESICLES - 1)
    return chosen.astype(jnp.int32)


def draw_cross_slots(key, part):
    rows = N_SECTOR * N_RADIAL
    scores = jax.random.randint(key, (rows, VES_DEV), 0, 1 << 20, dtype=jnp.int32) * VES_DEV
    scores = scores + jnp.arange(VES_DEV, dtype=jnp.int32)[None, :]
    scores = scores.at[0, 0].set(-1)
    scores = scores.at[rows - 1, VES_DEV - 1].set(-1)
    ordering = jnp.argsort(scores, axis=1)
    return ordering[:, :CROSS].astype(jnp.int32)


def shard_levels(own_key, extent, cuts, least, high):
    level = 1.0
    for dim, parts in cuts:
        heights = jax.random.uniform(jax.random.fold_in(jax.random.fold_in(own_key, 6), dim), (parts,), jnp.float32, least / len(cuts), high / len(cuts))
        level = level * jnp.repeat(jnp.exp(heights), extent[dim] // parts).reshape((-1,) + (1,) * (len(extent) - 1 - dim))
    return level


def centred(key, shape, spread, most, split=(), kind=jnp.bfloat16):
    gain = shard_levels(key, shape, split, -0.22, 0.18) if split else 1.0
    entries = jax.random.normal(key, shape, jnp.float32) * spread * gain
    return jnp.minimum(jnp.maximum(entries, -most), most).astype(kind)


def setup_inputs(seed: int = 0) -> dict:
    streams_of = jax.random.split(jax.random.key(seed), 7)
    return {
        "positions": centred(streams_of[0], (VESICLES, 2 * P_SIZE), 1.0, 6.0, ((0, 512),), jnp.float32),
        "stiffness": jnp.clip(jnp.exp(math.log(100.0) - 4.6051702 * jax.random.uniform(streams_of[1], (VESICLES,), jnp.float32) ** shard_levels(streams_of[1], (VESICLES,), ((0, 512),), -0.2, 0.2)), 1.0, 100.0),
        "blocks": centred(streams_of[2], (STEPS, PAIRS, 2 * P_SIZE, 2 * P_SIZE), (32 * P_SIZE) ** -0.5, 0.0625, ((1, 512),)),
        "pair_src": draw_pair_src(jax.random.fold_in(streams_of[6], 71), 0),
        "pair_tgt": draw_pair_tgt(jax.random.fold_in(streams_of[6], 71), 0),
        "cross_slots": draw_cross_slots(jax.random.fold_in(streams_of[6], 71), 0),
    }


epsilon = 1e-06

def bending_table(points):
    wavenumber = jnp.arange(points, dtype=jnp.int32)
    frequency = jnp.minimum(wavenumber, points - wavenumber).astype(jnp.float32)
    weights = (frequency / (points // 2)) ** 4 / points
    phases = wavenumber[:, None] * wavenumber[None, :] % points
    angles = phases.astype(jnp.float32) * (2.0 * math.pi / points)
    cosines = jnp.cos(angles)
    sines = jnp.sin(angles)
    return jnp.dot((cosines * weights[None, :]).astype(jnp.float32), cosines.T.astype(jnp.float32), preferred_element_type=jnp.float32, precision=lax.Precision.HIGHEST) + jnp.dot((sines * weights[None, :]).astype(jnp.float32), sines.T.astype(jnp.float32), preferred_element_type=jnp.float32, precision=lax.Precision.HIGHEST)

def apply_local(field, bending, fourth):
    rows = field.shape[0]
    shaped = field.reshape(rows * 2, -1)
    curved = jnp.dot(shaped.astype(jnp.float32), fourth.astype(jnp.float32), preferred_element_type=jnp.float32, precision=lax.Precision.HIGHEST).reshape(rows, -1)
    return field + bending[:, None] * curved

def near_terms(field, blocks, sources, targets):
    rounded = field.astype(jnp.bfloat16)
    gathered = rounded[sources]
    columns = field.shape[1]

    def one_owner(pieces):
        owner_blocks, owner_vectors = pieces
        return jnp.einsum('pij,pj->pi', owner_blocks.astype(jnp.float32), owner_vectors.astype(jnp.float32), precision=lax.Precision.HIGHEST)
    products = lax.map(one_owner, (blocks.reshape(-1, 3 * PAIR_OFF, columns, columns), gathered.reshape(-1, 3 * PAIR_OFF, columns)))
    products = products.reshape(-1, columns)
    return jax.ops.segment_sum(products, targets, num_segments=field.shape[0])

def gmres(rhs, bending, blocks, sources, targets, fourth):

    def operate(field):
        return apply_local(field, bending, fourth) + near_terms(field, blocks, sources, targets)
    first_norm = jnp.sqrt(jnp.sum(rhs * rhs) + epsilon)
    krylov = [rhs / first_norm]
    hessenberg = jnp.zeros((ITERS + 1, ITERS), jnp.float32)
    for column in range(ITERS):
        image = operate(krylov[column])
        project = jnp.stack([jnp.sum(vector * image) for vector in krylov])
        for inner in range(column + 1):
            image = image - project[inner] * krylov[inner]
        next_norm = jnp.sqrt(jnp.sum(image * image) + epsilon)
        hessenberg = hessenberg.at[:column + 1, column].set(project)
        hessenberg = hessenberg.at[column + 1, column].set(next_norm)
        krylov.append(image / next_norm)
    normal_matrix = jnp.dot(hessenberg.T.astype(jnp.float32), hessenberg.astype(jnp.float32), preferred_element_type=jnp.float32, precision=lax.Precision.HIGHEST)
    moment = first_norm * hessenberg[0]
    factor = jnp.linalg.cholesky(normal_matrix)
    coefficients = jax.scipy.linalg.cho_solve((factor, True), moment)
    result = coefficients[0] * krylov[0]
    for column in range(1, ITERS):
        result = result + coefficients[column] * krylov[column]
    return result

def reference(positions, stiffness, blocks, pair_src, pair_tgt, cross_slots):
    fourth = bending_table(P_SIZE)
    step_one = gmres(positions, stiffness, blocks[0], pair_src[0], pair_tgt[0], fourth)
    devices = cross_slots.shape[0]
    sectors = devices // N_RADIAL
    device_ids = jnp.arange(devices, dtype=jnp.int32)
    previous = (device_ids // N_RADIAL - 1) % sectors * N_RADIAL + device_ids % N_RADIAL
    target_rows = (device_ids[:, None] * VES_DEV + cross_slots).reshape(-1).astype(jnp.int32)
    source_rows = (previous[:, None] * VES_DEV + cross_slots[previous]).reshape(-1).astype(jnp.int32)
    after_crossing = step_one.at[target_rows].set(step_one[source_rows])
    moved_stiffness = stiffness.at[target_rows].set(stiffness[source_rows])
    final_positions = gmres(after_crossing, moved_stiffness, blocks[1], pair_src[1], pair_tgt[1], fourth)
    return (after_crossing, final_positions)
```

```python
import functools

import jax
import jax.numpy as jnp
import numpy as np
from jax import lax
from jax.experimental import pallas as pl
from jax.experimental.pallas import tpu as pltpu
from jax.sharding import Mesh
from jax.sharding import PartitionSpec as P

ITERS = 3
SECTOR = ("sector_0", "sector_1", "sector_2", "sector_3")
SECTOR_RADIAL = ("sector_0", "sector_1", "sector_2", "sector_3", "radial")
MESH = pl.DeviceIdType.MESH
EPSILON = 1e-06
GAMMA = 64.0
PAIRS_IN = 3
LINKS = 5


def bending_table(points):
    k = np.arange(points)
    weights = (np.minimum(k, points - k) / (points // 2)) ** 4 / points
    angles = (k[:, None] * k[None, :] % points) * (2.0 * np.pi / points)
    table = (np.cos(angles) * weights) @ np.cos(angles).T + (np.sin(angles) * weights) @ np.sin(angles).T
    return table.astype(np.float32)


def dot_nt(a, b, precision=None):
    return lax.dot_general(
        a, b, (((1,), (1,)), ((), ())), preferred_element_type=jnp.float32, precision=precision
    )


def total_of(terms):
    terms = list(terms)
    return functools.reduce(lambda a, b: a + b, terms)


def krylov_weights(gram):
    at = lambda i, j: gram[(min(i, j), max(i, j))]
    first = jnp.sqrt(at(0, 0) + EPSILON)
    basis = [[1.0 / first]]
    hess = {}
    for j in range(ITERS):
        image = [GAMMA * a for a in basis[j]]
        seen = [total_of(at(i, m + 1) * image[m] for m in range(j + 1)) for i in range(j + 1)]
        h = [total_of(basis[i][a] * seen[a] for a in range(i + 1)) for i in range(j + 1)]
        left = []
        for a in range(j + 2):
            value = image[a - 1] if a > 0 else None
            for i in range(a, j + 1):
                term = h[i] * basis[i][a]
                value = -term if value is None else value - term
            left.append(value)
        square = total_of(
            left[a] * total_of(at(a, b) * left[b] for b in range(j + 2)) for a in range(j + 2)
        )
        norm = jnp.sqrt(jnp.maximum(square, 0.0) + EPSILON)
        for i in range(j + 1):
            hess[(i, j)] = h[i]
        hess[(j + 1, j)] = norm
        scale = 1.0 / norm
        basis.append([a * scale for a in left])
    normal = {}
    for i in range(ITERS):
        for j in range(i + 1):
            normal[(i, j)] = total_of(hess[(k, i)] * hess[(k, j)] for k in range(min(i, j) + 2))
    moment = [first * hess[(0, j)] for j in range(ITERS)]
    factor, inverse = {}, []
    for i in range(ITERS):
        for j in range(i):
            value = normal[(i, j)]
            for k in range(j):
                value = value - factor[(i, k)] * factor[(j, k)]
            factor[(i, j)] = value * inverse[j]
        value = normal[(i, i)]
        for k in range(i):
            value = value - factor[(i, k)] * factor[(i, k)]
        inverse.append(1.0 / jnp.sqrt(value))
    forward = []
    for i in range(ITERS):
        value = moment[i]
        for k in range(i):
            value = value - factor[(i, k)] * forward[k]
        forward.append(value * inverse[i])
    coefficients = [None] * ITERS
    for i in reversed(range(ITERS)):
        value = forward[i]
        for k in range(i + 1, ITERS):
            value = value - factor[(k, i)] * coefficients[k]
        coefficients[i] = value * inverse[i]
    return [
        total_of(coefficients[j] * basis[j][a] for j in range(a, ITERS)) for a in range(ITERS)
    ]


def kernel(
    sizes,
    src_ref,
    tgt_ref,
    slot_ref,
    pos_ref,
    stiff_ref,
    fourth_ref,
    blocks_ref,
    after_ref,
    final_ref,
    block_buf,
    id_out,
    id_in,
    near_out,
    near_in,
    row_out,
    row_in,
    gram_buf,
    scalar_buf,
    sum_out,
    sum_in_0,
    sum_in_1,
    sum_in_2,
    block_sem,
    id_send,
    id_recv,
    near_send,
    near_recv,
    row_send,
    row_recv,
    sum_send,
    sum_recv,
):
    ny, nz, nx, nc, nr = sizes
    rows, columns = pos_ref.shape
    points = columns // 2
    y, z, x, c, r = (lax.axis_index(name) for name in SECTOR_RADIAL)
    sectors = ny * nz * nx * nc
    sector = ((y * nz + z) * nx + x) * nc + c
    own_base = (sector * nr + r) * rows

    def place(index, radial):
        return (
            lax.div(index, nc * nx * nz),
            lax.rem(lax.div(index, nc * nx), nz),
            lax.rem(lax.div(index, nc), nx),
            lax.rem(index, nc),
            radial,
        )

    before = lax.rem(sector + sectors - 1, sectors)
    after = lax.rem(sector + 1, sectors)
    other = lax.rem(r + 1, nr)
    links = [
        (0, place(before, r)),
        (0, place(before, other)),
        (1, (y, z, x, c, other)),
        (2, place(after, r)),
        (2, place(after, other)),
    ]

    stage_0 = [
        (lax.rem(x + i, nx), lax.rem(c + j, nc), lax.rem(r + k, nr))
        for i in range(nx)
        for j in range(nc)
        for k in range(nr)
    ][1:]
    stages = [
        [(y, z, a, b, d) for a, b, d in stage_0],
        [(lax.rem(y + i, ny), z, x, c, r) for i in range(1, ny)],
        [(y, lax.rem(z + i, nz), x, c, r) for i in range(1, nz)],
    ]

    loads = [
        pltpu.make_async_copy(blocks_ref.at[k], block_buf.at[k], block_sem.at[k]) for k in range(2)
    ]
    for load in loads:
        load.start()

    barrier = pltpu.get_barrier_semaphore()
    greeted = [device for _, device in links] + [device for stage in stages for device in stage]
    for device in greeted:
        pl.semaphore_signal(barrier, inc=1, device_id=device, device_id_type=MESH)

    lane = lax.broadcasted_iota(jnp.int32, (1, 128), 1)
    row_of = lax.broadcasted_iota(jnp.int32, (rows, 1), 0)
    row_wide = lax.broadcasted_iota(jnp.int32, (rows, columns), 0)
    eye = lax.broadcasted_iota(jnp.int32, (rows, rows), 0) == lax.broadcasted_iota(
        jnp.int32, (rows, rows), 1
    )
    stiff_row = stiff_ref[...]
    stiff = jnp.sum(jnp.where(eye, stiff_row, 0.0), axis=1, keepdims=True)
    slot = slot_ref[0, 0]
    leaving_stiff = jnp.sum(jnp.where(row_of == slot, stiff, 0.0), axis=0, keepdims=True)

    ids = jnp.where(lane == 6, leaving_stiff, 0.0)
    for k in range(2):
        for p in range(PAIRS_IN):
            ids = jnp.where(lane == k * PAIRS_IN + p, tgt_ref[k, p].astype(jnp.float32), ids)
    id_out[...] = ids

    pl.semaphore_wait(barrier, len(greeted))

    def send(source, target, send_sem, recv_sem, device):
        copy = pltpu.make_async_remote_copy(
            src_ref=source,
            dst_ref=target,
            send_sem=send_sem,
            recv_sem=recv_sem,
            device_id=device,
            device_id_type=MESH,
        )
        copy.start()
        return copy

    sent = []
    id_copies = [
        send(id_out, id_in.at[l], id_send.at[l], id_recv.at[l], device)
        for l, (_, device) in enumerate(links)
    ]
    sent += id_copies

    def targets_of(k):
        masks = []
        for l, (pair, _) in enumerate(links):
            target = jnp.sum(
                jnp.where(lane == k * PAIRS_IN + pair, id_in[l], 0.0), axis=1, keepdims=True
            )
            masks.append(row_of == target.astype(jnp.int32) - own_base)
        masks.append(row_of == tgt_ref[k, 1] - own_base)
        return [mask.astype(jnp.float32) for mask in masks]

    fourth = fourth_ref[...]
    operand_row = lax.broadcasted_iota(jnp.int32, (8, columns), 0)

    def apply(field, bending, k, exchange, masks):
        products = []
        for p in range(PAIRS_IN):
            source = src_ref[k, p] - own_base
            picked = jnp.sum(jnp.where(row_wide == source, field, 0.0), axis=0, keepdims=True)
            high = picked.astype(jnp.bfloat16).astype(jnp.float32)
            low = picked - high
            operand = jnp.where(
                operand_row == 0, high, jnp.where(operand_row == 1, low, 0.0)
            ).astype(jnp.bfloat16)
            product = jnp.sum(dot_nt(operand, block_buf[k, p]), axis=0, keepdims=True)
            near_out[exchange, p] = product
            products.append(product)
        copies = [
            send(
                near_out.at[exchange, pair],
                near_in.at[exchange, l],
                near_send.at[exchange, l],
                near_recv.at[exchange, l],
                device,
            )
            for l, (pair, device) in enumerate(links)
        ]
        sent.extend(copies)
        shaped = jnp.concatenate([field[:, :points], field[:, points:]], axis=0)
        curved = jnp.dot(
            shaped, fourth, preferred_element_type=jnp.float32, precision=lax.Precision.HIGHEST
        )
        curved = jnp.concatenate([curved[:rows], curved[rows:]], axis=1)
        image = field + bending * curved
        if masks is None:
            for copy in id_copies:
                copy.wait_recv()
            masks = targets_of(k)
        image = image + masks[LINKS] * products[1]
        for l, copy in enumerate(copies):
            copy.wait_recv()
            image = image + masks[l] * near_in[exchange, l]
        return image * (1.0 / GAMMA), masks

    def everywhere(values, which):
        for t, (stage, inbox) in enumerate(zip(stages, (sum_in_0, sum_in_1, sum_in_2))):
            if not stage:
                continue
            sum_out[which, t] = values
            first = sum(len(s) for s in stages[:t])
            copies = [
                send(
                    sum_out.at[which, t],
                    inbox.at[which, i],
                    sum_send.at[which, first + i],
                    sum_recv.at[which, first + i],
                    device,
                )
                for i, device in enumerate(stage)
            ]
            sent.extend(copies)
            for i, copy in enumerate(copies):
                copy.wait_recv()
                values = values + inbox[which, i]
        diagonal = lax.broadcasted_iota(jnp.int32, (128, 128), 0) == lax.broadcasted_iota(
            jnp.int32, (128, 128), 1
        )
        spread = jnp.dot(
            jnp.where(diagonal, values, 0.0),
            jnp.ones((128, 128), jnp.float32),
            preferred_element_type=jnp.float32,
            precision=lax.Precision.HIGHEST,
        )
        scalar_buf[...] = spread

    def folded(product):
        wide = sum(product[:, i * 128 : (i + 1) * 128] for i in range(columns // 128))
        return jnp.sum(wide, axis=0, keepdims=True)

    gram_buf[...] = jnp.zeros_like(gram_buf)

    def solve(start, bending, k, masks):
        basis = [start]
        for j in range(ITERS):
            image, masks = apply(basis[j], bending, k, k * ITERS + j, masks)
            basis.append(image)
        pairs = [(i, j) for i in range(ITERS + 1) for j in range(i, ITERS + 1)]
        for n, (i, j) in enumerate(pairs):
            gram_buf[n : n + 1, :] = folded(basis[i] * basis[j])
        sums = dot_nt(jnp.ones((8, 128), jnp.float32), gram_buf[...], lax.Precision.HIGHEST)
        everywhere(sums[0:1], k)
        weights = krylov_weights(
            {pair: scalar_buf[n : n + 1, :] for n, pair in enumerate(pairs)}
        )
        return total_of(
            jnp.broadcast_to(weights[a][:, 0:1], (rows, columns)) * basis[a] for a in range(ITERS)
        )

    for load in loads:
        load.wait()
    step_one = solve(pos_ref[...], stiff, 0, None)
    row_out[0] = jnp.sum(jnp.where(row_wide == slot, step_one, 0.0), axis=0, keepdims=True)
    crossing = send(row_out.at[0], row_in.at[0], row_send.at[0], row_recv.at[0], links[3][1])
    sent.append(crossing)
    masks = targets_of(1)
    new_stiff = jnp.sum(jnp.where(lane == 6, id_in[3], 0.0), axis=1, keepdims=True)
    moved_stiff = jnp.where(row_of == slot, new_stiff, stiff)
    crossing.wait_recv()
    crossed = jnp.where(row_wide == slot, row_in[0], step_one)
    after_ref[...] = crossed
    final_ref[...] = solve(crossed, moved_stiff, 1, masks)
    for copy in sent:
        copy.wait_send()


def local(sizes, table, positions, stiffness, blocks, pair_src, pair_tgt, cross_slots):
    rows, columns = positions.shape
    ny, nz, nx, nc, nr = sizes
    peers = (nx * nc * nr - 1, ny - 1, nz - 1)
    vmem = pl.BlockSpec(memory_space=pltpu.VMEM)
    smem = pl.BlockSpec(memory_space=pltpu.SMEM)
    f32 = jnp.float32
    dma = pltpu.SemaphoreType.DMA
    return pl.pallas_call(
        functools.partial(kernel, sizes),
        out_shape=(jax.ShapeDtypeStruct((rows, columns), f32),) * 2,
        in_specs=[smem, smem, smem, vmem, vmem, vmem, pl.BlockSpec(memory_space=pl.ANY)],
        out_specs=(vmem, vmem),
        scratch_shapes=[
            pltpu.VMEM(blocks.shape, blocks.dtype),
            pltpu.VMEM((1, 128), f32),
            pltpu.VMEM((LINKS, 1, 128), f32),
            pltpu.VMEM((2 * ITERS, PAIRS_IN, 1, columns), f32),
            pltpu.VMEM((2 * ITERS, LINKS, 1, columns), f32),
            pltpu.VMEM((1, 1, columns), f32),
            pltpu.VMEM((1, 1, columns), f32),
            pltpu.VMEM((128, 128), f32),
            pltpu.VMEM((128, 128), f32),
            pltpu.VMEM((2, 3, 1, 128), f32),
            pltpu.VMEM((2, max(peers[0], 1), 1, 128), f32),
            pltpu.VMEM((2, max(peers[1], 1), 1, 128), f32),
            pltpu.VMEM((2, max(peers[2], 1), 1, 128), f32),
            dma((2,)),
            dma((LINKS,)),
            dma((LINKS,)),
            dma((2 * ITERS, LINKS)),
            dma((2 * ITERS, LINKS)),
            dma((1,)),
            dma((1,)),
            dma((2, sum(peers))),
            dma((2, sum(peers))),
        ],
        compiler_params=pltpu.CompilerParams(collective_id=0, has_side_effects=True),
    )(
        pair_src,
        pair_tgt,
        cross_slots,
        positions,
        stiffness.reshape(1, rows),
        jnp.asarray(table),
        blocks,
    )


def program(split):
    sizes = tuple(split.shape[name] for name in SECTOR_RADIAL)
    placed = (
        P(SECTOR_RADIAL, None),
        P(SECTOR_RADIAL),
        P(None, SECTOR_RADIAL, None, None),
        P(None, SECTOR_RADIAL),
        P(None, SECTOR_RADIAL),
        P(SECTOR_RADIAL, None),
    )
    return jax.shard_map(
        functools.partial(local, sizes, bending_table(256)),
        mesh=split,
        in_specs=placed,
        out_specs=(P(SECTOR_RADIAL, None), P(SECTOR_RADIAL, None)),
        check_vma=False,
    )


def solution(mesh):
    split = Mesh(mesh.devices.reshape(4, 16, 2, 2, mesh.shape["radial"]), SECTOR_RADIAL)
    return program(split)
```

```python
import functools

import jax
import jax.numpy as jnp
import numpy as np
from jax import lax
from jax.experimental import pallas as pl
from jax.experimental.pallas import tpu as pltpu
from jax.sharding import Mesh
from jax.sharding import PartitionSpec as P

ITERS = 3
SECTOR = ("sector_0", "sector_1", "sector_2", "sector_3")
SECTOR_RADIAL = ("sector_0", "sector_1", "sector_2", "sector_3", "radial")
MESH = pl.DeviceIdType.MESH
EPSILON = 1e-06
GAMMA = 64.0
PAIRS_IN = 3
LINKS = 5


def bending_table(points):
    k = np.arange(points)
    weights = (np.minimum(k, points - k) / (points // 2)) ** 4 / points
    angles = (k[:, None] * k[None, :] % points) * (2.0 * np.pi / points)
    table = (np.cos(angles) * weights) @ np.cos(angles).T + (np.sin(angles) * weights) @ np.sin(angles).T
    return table.astype(np.float32)


def dot_nt(a, b, precision=None):
    return lax.dot_general(
        a, b, (((1,), (1,)), ((), ())), preferred_element_type=jnp.float32, precision=precision
    )


def total_of(terms):
    terms = list(terms)
    return functools.reduce(lambda a, b: a + b, terms)


def krylov_weights(gram):
    at = lambda i, j: gram[(min(i, j), max(i, j))]
    first = jnp.sqrt(at(0, 0) + EPSILON)
    basis = [[1.0 / first]]
    hess = {}
    for j in range(ITERS):
        image = [GAMMA * a for a in basis[j]]
        seen = [total_of(at(i, m + 1) * image[m] for m in range(j + 1)) for i in range(j + 1)]
        h = [total_of(basis[i][a] * seen[a] for a in range(i + 1)) for i in range(j + 1)]
        left = []
        for a in range(j + 2):
            value = image[a - 1] if a > 0 else None
            for i in range(a, j + 1):
                term = h[i] * basis[i][a]
                value = -term if value is None else value - term
            left.append(value)
        square = total_of(
            left[a] * total_of(at(a, b) * left[b] for b in range(j + 2)) for a in range(j + 2)
        )
        norm = jnp.sqrt(jnp.maximum(square, 0.0) + EPSILON)
        for i in range(j + 1):
            hess[(i, j)] = h[i]
        hess[(j + 1, j)] = norm
        scale = 1.0 / norm
        basis.append([a * scale for a in left])
    normal = {}
    for i in range(ITERS):
        for j in range(i + 1):
            normal[(i, j)] = total_of(hess[(k, i)] * hess[(k, j)] for k in range(min(i, j) + 2))
    moment = [first * hess[(0, j)] for j in range(ITERS)]
    factor, inverse = {}, []
    for i in range(ITERS):
        for j in range(i):
            value = normal[(i, j)]
            for k in range(j):
                value = value - factor[(i, k)] * factor[(j, k)]
            factor[(i, j)] = value * inverse[j]
        value = normal[(i, i)]
        for k in range(i):
            value = value - factor[(i, k)] * factor[(i, k)]
        inverse.append(1.0 / jnp.sqrt(value))
    forward = []
    for i in range(ITERS):
        value = moment[i]
        for k in range(i):
            value = value - factor[(i, k)] * forward[k]
        forward.append(value * inverse[i])
    coefficients = [None] * ITERS
    for i in reversed(range(ITERS)):
        value = forward[i]
        for k in range(i + 1, ITERS):
            value = value - factor[(k, i)] * coefficients[k]
        coefficients[i] = value * inverse[i]
    return [
        total_of(coefficients[j] * basis[j][a] for j in range(a, ITERS)) for a in range(ITERS)
    ]


def kernel(
    sizes,
    src_ref,
    tgt_ref,
    slot_ref,
    pos_ref,
    stiff_ref,
    fourth_ref,
    blocks_ref,
    after_ref,
    final_ref,
    block_buf,
    id_out,
    id_in,
    near_out,
    near_in,
    wide_out,
    wide_in,
    row_out,
    row_in,
    gram_buf,
    scalar_buf,
    sum_out,
    sum_in_0,
    sum_in_1,
    sum_in_2,
    block_sem,
    id_send,
    id_recv,
    near_send,
    near_recv,
    row_send,
    row_recv,
    sum_send,
    sum_recv,
):
    ny, nz, nx, nc, nr = sizes
    rows, columns = pos_ref.shape
    points = columns // 2
    y, z, x, c, r = (lax.axis_index(name) for name in SECTOR_RADIAL)
    sectors = ny * nz * nx * nc
    sector = ((y * nz + z) * nx + x) * nc + c
    own_base = (sector * nr + r) * rows

    def place(index, radial):
        return (
            lax.div(index, nc * nx * nz),
            lax.rem(lax.div(index, nc * nx), nz),
            lax.rem(lax.div(index, nc), nx),
            lax.rem(index, nc),
            radial,
        )

    before = lax.rem(sector + sectors - 1, sectors)
    after = lax.rem(sector + 1, sectors)
    other = lax.rem(r + 1, nr)
    links = [
        (0, place(before, r)),
        (0, place(before, other)),
        (1, (y, z, x, c, other)),
        (2, place(after, r)),
        (2, place(after, other)),
    ]

    stage_0 = [
        (lax.rem(x + i, nx), lax.rem(c + j, nc), lax.rem(r + k, nr))
        for i in range(nx)
        for j in range(nc)
        for k in range(nr)
    ][1:]
    stages = [
        [(y, z, a, b, d) for a, b, d in stage_0],
        [(lax.rem(y + i, ny), z, x, c, r) for i in range(1, ny)],
        [(y, lax.rem(z + i, nz), x, c, r) for i in range(1, nz)],
    ]

    loads = [
        pltpu.make_async_copy(blocks_ref.at[k], block_buf.at[k], block_sem.at[k]) for k in range(2)
    ]
    for load in loads:
        load.start()

    barrier = pltpu.get_barrier_semaphore()
    greeted = [device for _, device in links] + [device for stage in stages for device in stage]
    for device in greeted:
        pl.semaphore_signal(barrier, inc=1, device_id=device, device_id_type=MESH)

    lane = lax.broadcasted_iota(jnp.int32, (1, 128), 1)
    row_of = lax.broadcasted_iota(jnp.int32, (rows, 1), 0)
    row_wide = lax.broadcasted_iota(jnp.int32, (rows, columns), 0)
    eye = lax.broadcasted_iota(jnp.int32, (rows, rows), 0) == lax.broadcasted_iota(
        jnp.int32, (rows, rows), 1
    )
    stiff_row = stiff_ref[...]
    stiff = jnp.sum(jnp.where(eye, stiff_row, 0.0), axis=1, keepdims=True)
    slot = slot_ref[0, 0]
    leaving_stiff = jnp.sum(jnp.where(row_of == slot, stiff, 0.0), axis=0, keepdims=True)

    ids = jnp.where(lane == 6, leaving_stiff, 0.0)
    for k in range(2):
        for p in range(PAIRS_IN):
            ids = jnp.where(lane == k * PAIRS_IN + p, tgt_ref[k, p].astype(jnp.float32), ids)
    id_out[...] = ids

    def send(source, target, send_sem, recv_sem, device):
        copy = pltpu.make_async_remote_copy(
            src_ref=source,
            dst_ref=target,
            send_sem=send_sem,
            recv_sem=recv_sem,
            device_id=device,
            device_id_type=MESH,
        )
        copy.start()
        return copy

    sent = []
    def targets_of(k):
        masks = []
        for l, (pair, _) in enumerate(links):
            target = jnp.sum(
                jnp.where(lane == k * PAIRS_IN + pair, id_in[l], 0.0), axis=1, keepdims=True
            )
            masks.append(row_of == target.astype(jnp.int32) - own_base)
        masks.append(row_of == tgt_ref[k, 1] - own_base)
        return [mask.astype(jnp.float32) for mask in masks]

    fourth = fourth_ref[...]
    operand_row = lax.broadcasted_iota(jnp.int32, (8, columns), 0)

    def pick(fields, k, exchange):
        out = near_out.at[exchange] if len(fields) == 1 else wide_out.at[exchange - ITERS]
        own = None
        for p in range(PAIRS_IN):
            mask = row_wide == src_ref[k, p] - own_base
            stacked = jnp.zeros((8, columns), jnp.float32)
            for j, field in enumerate(fields):
                picked = jnp.sum(jnp.where(mask, field, 0.0), axis=0, keepdims=True)
                stacked = jnp.where(lax.rem(operand_row, 4) == j, picked, stacked)
            high = stacked.astype(jnp.bfloat16).astype(jnp.float32)
            operand = jnp.where(operand_row < 4, high, stacked - high).astype(jnp.bfloat16)
            product = dot_nt(operand, block_buf[k, p])
            product = product[0:4] + product[4:8]
            if len(fields) == 1:
                product = product[0:1]
            out[p] = product
            if p == 1:
                own = product
        return own

    def launch(exchange):
        wide = exchange >= ITERS
        source = wide_out.at[exchange - ITERS] if wide else near_out.at[exchange]
        target = wide_in.at[exchange - ITERS] if wide else near_in.at[exchange]
        copies = [
            send(
                source.at[pair],
                target.at[l],
                near_send.at[exchange, l],
                near_recv.at[exchange, l],
                device,
            )
            for l, (pair, device) in enumerate(links)
        ]
        sent.extend(copies)
        return copies

    def bend(fields, bending):
        halves = [f[:, i * points : (i + 1) * points] for f in fields for i in range(2)]
        curved = jnp.dot(
            jnp.concatenate(halves, axis=0),
            fourth,
            preferred_element_type=jnp.float32,
            precision=lax.Precision.HIGHEST,
        )
        images = []
        for j, field in enumerate(fields):
            x_part = curved[2 * j * rows : (2 * j + 1) * rows]
            y_part = curved[(2 * j + 1) * rows : (2 * j + 2) * rows]
            images.append(field + bending * jnp.concatenate([x_part, y_part], axis=1))
        return images

    def receive(images, own, copies, exchange, masks):
        wide = exchange >= ITERS
        images = [image + masks[LINKS] * own[j : j + 1] for j, image in enumerate(images)]
        for l, copy in enumerate(copies):
            copy.wait_recv()
            arrived = wide_in[exchange - ITERS, l] if wide else near_in[exchange, l]
            images = [
                image + masks[l] * arrived[j : j + 1] for j, image in enumerate(images)
            ]
        return [image * (1.0 / GAMMA) for image in images]

    def folded(product):
        wide = total_of(product[:, i * 128 : (i + 1) * 128] for i in range(columns // 128))
        return jnp.sum(wide, axis=0, keepdims=True)

    gram_pairs = [(i, j) for i in range(ITERS + 1) for j in range(i, ITERS + 1)]

    def gram_sums(basis):
        for n, (i, j) in enumerate(gram_pairs):
            gram_buf[n : n + 1, :] = folded(basis[i] * basis[j])
        sums = dot_nt(jnp.ones((8, 128), jnp.float32), gram_buf[...], lax.Precision.HIGHEST)
        return sums[0:1]

    order = [2, 0, 1]
    inboxes = (sum_in_0, sum_in_1, sum_in_2)

    def stage_start(values, which, t):
        stage, inbox = stages[t], inboxes[t]
        first = sum(len(s) for s in stages[:t])
        sum_out[which, t] = values
        copies = [
            send(
                sum_out.at[which, t],
                inbox.at[which, i],
                sum_send.at[which, first + i],
                sum_recv.at[which, first + i],
                device,
            )
            for i, device in enumerate(stage)
        ]
        sent.extend(copies)
        return copies

    def stage_end(values, copies, which, t):
        for i, copy in enumerate(copies):
            copy.wait_recv()
            values = values + inboxes[t][which, i]
        return values

    def weights_of(values):
        diagonal = lax.broadcasted_iota(jnp.int32, (128, 128), 0) == lax.broadcasted_iota(
            jnp.int32, (128, 128), 1
        )
        scalar_buf[...] = jnp.dot(
            jnp.where(diagonal, values, 0.0),
            jnp.ones((128, 128), jnp.float32),
            preferred_element_type=jnp.float32,
            precision=lax.Precision.HIGHEST,
        )
        weights = krylov_weights(
            {pair: scalar_buf[n : n + 1, :] for n, pair in enumerate(gram_pairs)}
        )
        return [jnp.broadcast_to(weight[:, 0:1], (rows, columns)) for weight in weights]

    def cross(field, j):
        row_out[j] = jnp.sum(jnp.where(row_wide == slot, field, 0.0), axis=0, keepdims=True)
        copy = send(row_out.at[j], row_in.at[j], row_send.at[j], row_recv.at[j], links[3][1])
        sent.append(copy)
        return copy

    gram_buf[...] = jnp.zeros_like(gram_buf)
    start = pos_ref[...]
    loads[0].wait()
    own = pick([start], 0, 0)
    images = bend([start], stiff)

    pl.semaphore_wait(barrier, len(greeted))
    copies = launch(0)
    id_copies = [
        send(id_out, id_in.at[l], id_send.at[l], id_recv.at[l], device)
        for l, (_, device) in enumerate(links)
    ]
    sent += id_copies
    crossings = [cross(start, 0)]
    loads[1].wait()
    for copy in id_copies:
        copy.wait_recv()
    masks = targets_of(0)
    later_masks = targets_of(1)
    new_stiff = jnp.sum(jnp.where(lane == 6, id_in[3], 0.0), axis=1, keepdims=True)
    moved_stiff = jnp.where(row_of == slot, new_stiff, stiff)

    basis = [start] + receive(images, own, copies, 0, masks)
    for j in range(1, ITERS):
        own = pick([basis[j]], 0, j)
        copies = launch(j)
        crossings.append(cross(basis[j], j))
        images = bend([basis[j]], stiff)
        basis += receive(images, own, copies, j, masks)

    level = []
    for j in range(ITERS):
        crossings[j].wait_recv()
        level.append(jnp.where(row_wide == slot, row_in[j], basis[j]))
    levels = [level]
    flying = None
    for j in range(ITERS):
        exchange = ITERS + j
        own = pick(levels[j], 1, exchange)
        copies = launch(exchange)
        values = gram_sums(basis) if j == 0 else stage_end(values, flying, 0, order[j - 1])
        flying = stage_start(values, 0, order[j])
        images = bend(levels[j], moved_stiff)
        levels.append(receive(images, own, copies, exchange, later_masks))
    values = stage_end(values, flying, 0, order[ITERS - 1])
    weights = weights_of(values)
    second = [total_of(w * part for w, part in zip(weights, parts)) for parts in levels]
    after_ref[...] = second[0]
    values = gram_sums(second)
    for t in order:
        values = stage_end(values, stage_start(values, 1, t), 1, t)
    weights = weights_of(values)
    final_ref[...] = total_of(w * part for w, part in zip(weights, second))
    for copy in sent:
        copy.wait_send()


def local(sizes, table, positions, stiffness, blocks, pair_src, pair_tgt, cross_slots):
    rows, columns = positions.shape
    ny, nz, nx, nc, nr = sizes
    peers = (nx * nc * nr - 1, ny - 1, nz - 1)
    vmem = pl.BlockSpec(memory_space=pltpu.VMEM)
    smem = pl.BlockSpec(memory_space=pltpu.SMEM)
    f32 = jnp.float32
    dma = pltpu.SemaphoreType.DMA
    return pl.pallas_call(
        functools.partial(kernel, sizes),
        out_shape=(jax.ShapeDtypeStruct((rows, columns), f32),) * 2,
        in_specs=[smem, smem, smem, vmem, vmem, vmem, pl.BlockSpec(memory_space=pl.ANY)],
        out_specs=(vmem, vmem),
        scratch_shapes=[
            pltpu.VMEM(blocks.shape, blocks.dtype),
            pltpu.VMEM((1, 128), f32),
            pltpu.VMEM((LINKS, 1, 128), f32),
            pltpu.VMEM((ITERS, PAIRS_IN, 1, columns), f32),
            pltpu.VMEM((ITERS, LINKS, 1, columns), f32),
            pltpu.VMEM((ITERS, PAIRS_IN, 4, columns), f32),
            pltpu.VMEM((ITERS, LINKS, 4, columns), f32),
            pltpu.VMEM((ITERS, 1, columns), f32),
            pltpu.VMEM((ITERS, 1, columns), f32),
            pltpu.VMEM((128, 128), f32),
            pltpu.VMEM((128, 128), f32),
            pltpu.VMEM((2, 3, 1, 128), f32),
            pltpu.VMEM((2, max(peers[0], 1), 1, 128), f32),
            pltpu.VMEM((2, max(peers[1], 1), 1, 128), f32),
            pltpu.VMEM((2, max(peers[2], 1), 1, 128), f32),
            dma((2,)),
            dma((LINKS,)),
            dma((LINKS,)),
            dma((2 * ITERS, LINKS)),
            dma((2 * ITERS, LINKS)),
            dma((ITERS,)),
            dma((ITERS,)),
            dma((2, sum(peers))),
            dma((2, sum(peers))),
        ],
        compiler_params=pltpu.CompilerParams(collective_id=0, has_side_effects=True),
    )(
        pair_src,
        pair_tgt,
        cross_slots,
        positions,
        stiffness.reshape(1, rows),
        jnp.asarray(table),
        blocks,
    )


def program(split):
    sizes = tuple(split.shape[name] for name in SECTOR_RADIAL)
    placed = (
        P(SECTOR_RADIAL, None),
        P(SECTOR_RADIAL),
        P(None, SECTOR_RADIAL, None, None),
        P(None, SECTOR_RADIAL),
        P(None, SECTOR_RADIAL),
        P(SECTOR_RADIAL, None),
    )
    return jax.shard_map(
        functools.partial(local, sizes, bending_table(256)),
        mesh=split,
        in_specs=placed,
        out_specs=(P(SECTOR_RADIAL, None), P(SECTOR_RADIAL, None)),
        check_vma=False,
    )


def solution(mesh):
    split = Mesh(mesh.devices.reshape(4, 16, 2, 2, mesh.shape["radial"]), SECTOR_RADIAL)
    return program(split)
```

```python
import functools

import jax
import jax.numpy as jnp
import numpy as np
from jax import lax
from jax.experimental import pallas as pl
from jax.experimental.pallas import tpu as pltpu
from jax.sharding import Mesh
from jax.sharding import PartitionSpec as P

ITERS = 3
SECTOR = ("sector_0", "sector_1", "sector_2", "sector_3")
SECTOR_RADIAL = ("sector_0", "sector_1", "sector_2", "sector_3", "radial")
MESH = pl.DeviceIdType.MESH
EPSILON = 1e-06
GAMMA = 64.0
PAIRS_IN = 3
LINKS = 5


def bending_table(points):
    k = np.arange(points)
    weights = (np.minimum(k, points - k) / (points // 2)) ** 4 / points
    angles = (k[:, None] * k[None, :] % points) * (2.0 * np.pi / points)
    table = (np.cos(angles) * weights) @ np.cos(angles).T + (np.sin(angles) * weights) @ np.sin(angles).T
    return table.astype(np.float32)


def dot_nt(a, b, precision=None):
    return lax.dot_general(
        a, b, (((1,), (1,)), ((), ())), preferred_element_type=jnp.float32, precision=precision
    )


def total_of(terms):
    terms = list(terms)
    return functools.reduce(lambda a, b: a + b, terms)


def krylov_weights(gram):
    at = lambda i, j: gram[(min(i, j), max(i, j))]
    first = jnp.sqrt(at(0, 0) + EPSILON)
    basis = [[1.0 / first]]
    hess = {}
    for j in range(ITERS):
        image = [GAMMA * a for a in basis[j]]
        seen = [total_of(at(i, m + 1) * image[m] for m in range(j + 1)) for i in range(j + 1)]
        h = [total_of(basis[i][a] * seen[a] for a in range(i + 1)) for i in range(j + 1)]
        left = []
        for a in range(j + 2):
            value = image[a - 1] if a > 0 else None
            for i in range(a, j + 1):
                term = h[i] * basis[i][a]
                value = -term if value is None else value - term
            left.append(value)
        square = total_of(
            left[a] * total_of(at(a, b) * left[b] for b in range(j + 2)) for a in range(j + 2)
        )
        norm = jnp.sqrt(jnp.maximum(square, 0.0) + EPSILON)
        for i in range(j + 1):
            hess[(i, j)] = h[i]
        hess[(j + 1, j)] = norm
        scale = 1.0 / norm
        basis.append([a * scale for a in left])
    normal = {}
    for i in range(ITERS):
        for j in range(i + 1):
            normal[(i, j)] = total_of(hess[(k, i)] * hess[(k, j)] for k in range(min(i, j) + 2))
    moment = [first * hess[(0, j)] for j in range(ITERS)]
    factor, inverse = {}, []
    for i in range(ITERS):
        for j in range(i):
            value = normal[(i, j)]
            for k in range(j):
                value = value - factor[(i, k)] * factor[(j, k)]
            factor[(i, j)] = value * inverse[j]
        value = normal[(i, i)]
        for k in range(i):
            value = value - factor[(i, k)] * factor[(i, k)]
        inverse.append(1.0 / jnp.sqrt(value))
    forward = []
    for i in range(ITERS):
        value = moment[i]
        for k in range(i):
            value = value - factor[(i, k)] * forward[k]
        forward.append(value * inverse[i])
    coefficients = [None] * ITERS
    for i in reversed(range(ITERS)):
        value = forward[i]
        for k in range(i + 1, ITERS):
            value = value - factor[(k, i)] * coefficients[k]
        coefficients[i] = value * inverse[i]
    return [
        total_of(coefficients[j] * basis[j][a] for j in range(a, ITERS)) for a in range(ITERS)
    ]


def kernel(
    sizes,
    src_any,
    tgt_any,
    slot_any,
    pos_any,
    stiff_any,
    fourth_any,
    blocks_ref,
    after_ref,
    final_ref,
    src_ref,
    tgt_ref,
    slot_ref,
    pos_ref,
    stiff_ref,
    fourth_ref,
    block_buf,
    id_out,
    id_in,
    near_out,
    near_in,
    wide_out,
    wide_in,
    row_out,
    row_in,
    gram_buf,
    scalar_buf,
    sum_out,
    sum_in_0,
    sum_in_1,
    sum_in_2,
    load_sem,
    block_sem,
    ready_sem,
    id_send,
    id_recv,
    near_send,
    near_recv,
    row_send,
    row_recv,
    sum_send,
    sum_recv,
):
    ny, nz, nx, nc, nr = sizes
    rows, columns = pos_ref.shape
    points = columns // 2
    y, z, x, c, r = (lax.axis_index(name) for name in SECTOR_RADIAL)
    sectors = ny * nz * nx * nc
    sector = ((y * nz + z) * nx + x) * nc + c
    own_base = (sector * nr + r) * rows

    def place(index, radial):
        return (
            lax.div(index, nc * nx * nz),
            lax.rem(lax.div(index, nc * nx), nz),
            lax.rem(lax.div(index, nc), nx),
            lax.rem(index, nc),
            radial,
        )

    before = lax.rem(sector + sectors - 1, sectors)
    after = lax.rem(sector + 1, sectors)
    other = lax.rem(r + 1, nr)
    links = [
        (0, place(before, r)),
        (0, place(before, other)),
        (1, (y, z, x, c, other)),
        (2, place(after, r)),
        (2, place(after, other)),
    ]

    stage_0 = [
        (lax.rem(x + i, nx), lax.rem(c + j, nc), lax.rem(r + k, nr))
        for i in range(nx)
        for j in range(nc)
        for k in range(nr)
    ][1:]
    stages = [
        [(y, z, a, b, d) for a, b, d in stage_0],
        [(lax.rem(y + i, ny), z, x, c, r) for i in range(1, ny)],
        [(y, lax.rem(z + i, nz), x, c, r) for i in range(1, nz)],
    ]

    def around(distance):
        steps = sorted({distance % nz, -distance % nz} - {0})
        return [(y, lax.rem(z + step, nz), x, c, r) for step in steps]

    barrier = pltpu.get_barrier_semaphore()
    greeted = [device for _, device in links] + stages[0] + stages[1] + around(1)
    for device in greeted:
        pl.semaphore_signal(barrier, inc=1, device_id=device, device_id_type=MESH)

    small = [
        pltpu.make_async_copy(source, target, load_sem.at[n])
        for n, (source, target) in enumerate(
            (
                (src_any, src_ref),
                (tgt_any, tgt_ref),
                (slot_any, slot_ref),
                (stiff_any, stiff_ref),
                (pos_any, pos_ref),
                (fourth_any, fourth_ref),
            )
        )
    ]
    loads = [
        pltpu.make_async_copy(blocks_ref.at[k], block_buf.at[k], block_sem.at[k]) for k in range(2)
    ]
    for load in small + loads:
        load.start()

    reach = [1]
    while 2 * reach[-1] < nz:
        reach.append(2 * reach[-1])
    reach = reach[:-1] if len(reach) > 1 else []

    def tell(n):
        for device in around(reach[n]):
            pl.semaphore_signal(
                ready_sem.at[n], inc=1, device_id=device, device_id_type=MESH
            )

    def hear(n):
        pl.semaphore_wait(ready_sem.at[n], len(around(reach[n])))

    for load in small:
        load.wait()

    lane = lax.broadcasted_iota(jnp.int32, (1, 128), 1)
    row_of = lax.broadcasted_iota(jnp.int32, (rows, 1), 0)
    row_wide = lax.broadcasted_iota(jnp.int32, (rows, columns), 0)
    eye = lax.broadcasted_iota(jnp.int32, (rows, rows), 0) == lax.broadcasted_iota(
        jnp.int32, (rows, rows), 1
    )
    stiff_row = stiff_ref[...]
    stiff = jnp.sum(jnp.where(eye, stiff_row, 0.0), axis=1, keepdims=True)
    slot = slot_ref[...]
    leaving_stiff = jnp.sum(jnp.where(row_of == slot, stiff, 0.0), axis=0, keepdims=True)

    pair_at = [lax.broadcasted_iota(jnp.int32, (2, PAIRS_IN), axis) for axis in range(2)]

    def entry(ref, k, p):
        chosen = (pair_at[0] == k) & (pair_at[1] == p)
        row = jnp.sum(jnp.where(chosen, ref[...].astype(jnp.float32), 0.0), axis=1, keepdims=True)
        return jnp.sum(row, axis=0, keepdims=True)

    targets = {(k, p): entry(tgt_ref, k, p) for k in range(2) for p in range(PAIRS_IN)}
    sources = {
        (k, p): entry(src_ref, k, p).astype(jnp.int32) - own_base
        for k in range(2)
        for p in range(PAIRS_IN)
    }
    ids = jnp.where(lane == 6, leaving_stiff, 0.0)
    for k in range(2):
        for p in range(PAIRS_IN):
            ids = jnp.where(lane == k * PAIRS_IN + p, targets[k, p], ids)
    id_out[...] = ids

    def send(source, target, send_sem, recv_sem, device):
        copy = pltpu.make_async_remote_copy(
            src_ref=source,
            dst_ref=target,
            send_sem=send_sem,
            recv_sem=recv_sem,
            device_id=device,
            device_id_type=MESH,
        )
        copy.start()
        return copy

    sent = []
    def targets_of(k):
        masks = []
        for l, (pair, _) in enumerate(links):
            target = jnp.sum(
                jnp.where(lane == k * PAIRS_IN + pair, id_in[l], 0.0), axis=1, keepdims=True
            )
            masks.append(row_of == target.astype(jnp.int32) - own_base)
        masks.append(row_of == targets[k, 1].astype(jnp.int32) - own_base)
        return [mask.astype(jnp.float32) for mask in masks]

    fourth = fourth_ref[...]
    operand_row = lax.broadcasted_iota(jnp.int32, (8, columns), 0)

    def pick(fields, k, exchange):
        out = near_out.at[exchange] if len(fields) == 1 else wide_out.at[exchange - ITERS]
        own = None
        for p in range(PAIRS_IN):
            mask = row_wide == sources[k, p]
            stacked = jnp.zeros((8, columns), jnp.float32)
            for j, field in enumerate(fields):
                picked = jnp.sum(jnp.where(mask, field, 0.0), axis=0, keepdims=True)
                stacked = jnp.where(lax.rem(operand_row, 4) == j, picked, stacked)
            high = stacked.astype(jnp.bfloat16).astype(jnp.float32)
            operand = jnp.where(operand_row < 4, high, stacked - high).astype(jnp.bfloat16)
            product = dot_nt(operand, block_buf[k, p])
            product = product[0:4] + product[4:8]
            if len(fields) == 1:
                product = product[0:1]
            out[p] = product
            if p == 1:
                own = product
        return own

    def launch(exchange):
        wide = exchange >= ITERS
        source = wide_out.at[exchange - ITERS] if wide else near_out.at[exchange]
        target = wide_in.at[exchange - ITERS] if wide else near_in.at[exchange]
        copies = [
            send(
                source.at[pair],
                target.at[l],
                near_send.at[exchange, l],
                near_recv.at[exchange, l],
                device,
            )
            for l, (pair, device) in enumerate(links)
        ]
        sent.extend(copies)
        return copies

    def bend(fields, bending):
        halves = [f[:, i * points : (i + 1) * points] for f in fields for i in range(2)]
        curved = jnp.dot(
            jnp.concatenate(halves, axis=0),
            fourth,
            preferred_element_type=jnp.float32,
            precision=lax.Precision.HIGHEST,
        )
        images = []
        for j, field in enumerate(fields):
            x_part = curved[2 * j * rows : (2 * j + 1) * rows]
            y_part = curved[(2 * j + 1) * rows : (2 * j + 2) * rows]
            images.append(field + bending * jnp.concatenate([x_part, y_part], axis=1))
        return images

    def receive(images, own, copies, exchange, masks):
        wide = exchange >= ITERS
        images = [image + masks[LINKS] * own[j : j + 1] for j, image in enumerate(images)]
        for l, copy in enumerate(copies):
            copy.wait_recv()
            arrived = wide_in[exchange - ITERS, l] if wide else near_in[exchange, l]
            images = [
                image + masks[l] * arrived[j : j + 1] for j, image in enumerate(images)
            ]
        return [image * (1.0 / GAMMA) for image in images]

    def folded(product):
        wide = total_of(product[:, i * 128 : (i + 1) * 128] for i in range(columns // 128))
        return jnp.sum(wide, axis=0, keepdims=True)

    gram_pairs = [(i, j) for i in range(ITERS + 1) for j in range(i, ITERS + 1)]

    def gram_sums(basis):
        for n, (i, j) in enumerate(gram_pairs):
            gram_buf[n : n + 1, :] = folded(basis[i] * basis[j])
        sums = dot_nt(jnp.ones((8, 128), jnp.float32), gram_buf[...], lax.Precision.HIGHEST)
        return sums[0:1]

    order = [2, 0, 1]
    inboxes = (sum_in_0, sum_in_1, sum_in_2)

    def stage_start(values, which, t):
        stage, inbox = stages[t], inboxes[t]
        first = sum(len(s) for s in stages[:t])
        sum_out[which, t] = values
        copies = [
            send(
                sum_out.at[which, t],
                inbox.at[which, i],
                sum_send.at[which, first + i],
                sum_recv.at[which, first + i],
                device,
            )
            for i, device in enumerate(stage)
        ]
        sent.extend(copies)
        return copies

    def stage_end(values, copies, which, t):
        for i, copy in enumerate(copies):
            copy.wait_recv()
            values = values + inboxes[t][which, i]
        return values

    def weights_of(values):
        diagonal = lax.broadcasted_iota(jnp.int32, (128, 128), 0) == lax.broadcasted_iota(
            jnp.int32, (128, 128), 1
        )
        scalar_buf[...] = jnp.dot(
            jnp.where(diagonal, values, 0.0),
            jnp.ones((128, 128), jnp.float32),
            preferred_element_type=jnp.float32,
            precision=lax.Precision.HIGHEST,
        )
        weights = krylov_weights(
            {pair: scalar_buf[n : n + 1, :] for n, pair in enumerate(gram_pairs)}
        )
        return [jnp.broadcast_to(weight[:, 0:1], (rows, columns)) for weight in weights]

    def cross(field, j):
        row_out[j] = jnp.sum(jnp.where(row_wide == slot, field, 0.0), axis=0, keepdims=True)
        copy = send(row_out.at[j], row_in.at[j], row_send.at[j], row_recv.at[j], links[3][1])
        sent.append(copy)
        return copy

    gram_buf[...] = jnp.zeros_like(gram_buf)
    start = pos_ref[...]
    loads[0].wait()
    own = pick([start], 0, 0)
    images = bend([start], stiff)

    pl.semaphore_wait(barrier, len(greeted))
    copies = launch(0)
    id_copies = [
        send(id_out, id_in.at[l], id_send.at[l], id_recv.at[l], device)
        for l, (_, device) in enumerate(links)
    ]
    sent += id_copies
    if reach:
        tell(0)
    crossings = [cross(start, 0)]
    loads[1].wait()
    for copy in id_copies:
        copy.wait_recv()
    masks = targets_of(0)
    later_masks = targets_of(1)
    new_stiff = jnp.sum(jnp.where(lane == 6, id_in[3], 0.0), axis=1, keepdims=True)
    moved_stiff = jnp.where(row_of == slot, new_stiff, stiff)

    basis = [start] + receive(images, own, copies, 0, masks)
    for j in range(1, ITERS):
        own = pick([basis[j]], 0, j)
        copies = launch(j)
        crossings.append(cross(basis[j], j))
        if j - 1 < len(reach):
            hear(j - 1)
            if j < len(reach):
                tell(j)
        images = bend([basis[j]], stiff)
        basis += receive(images, own, copies, j, masks)

    for n in range(ITERS - 1, len(reach)):
        hear(n)
        if n + 1 < len(reach):
            tell(n + 1)
    level = []
    for j in range(ITERS):
        crossings[j].wait_recv()
        level.append(jnp.where(row_wide == slot, row_in[j], basis[j]))
    levels = [level]
    flying = None
    for j in range(ITERS):
        exchange = ITERS + j
        own = pick(levels[j], 1, exchange)
        copies = launch(exchange)
        values = gram_sums(basis) if j == 0 else stage_end(values, flying, 0, order[j - 1])
        flying = stage_start(values, 0, order[j])
        images = bend(levels[j], moved_stiff)
        levels.append(receive(images, own, copies, exchange, later_masks))
    values = stage_end(values, flying, 0, order[ITERS - 1])
    weights = weights_of(values)
    second = [total_of(w * part for w, part in zip(weights, parts)) for parts in levels]
    after_ref[...] = second[0]
    values = gram_sums(second)
    for t in order:
        values = stage_end(values, stage_start(values, 1, t), 1, t)
    weights = weights_of(values)
    final_ref[...] = total_of(w * part for w, part in zip(weights, second))
    for copy in sent:
        copy.wait_send()


def hand_over(after_in, final_in, after_ref, final_ref):
    after_ref[...] = after_in[...]
    final_ref[...] = final_in[...]


def local(sizes, table, positions, stiffness, blocks, pair_src, pair_tgt, cross_slots):
    rows, columns = positions.shape
    ny, nz, nx, nc, nr = sizes
    peers = (nx * nc * nr - 1, ny - 1, nz - 1)
    vmem = pl.BlockSpec(memory_space=pltpu.VMEM)
    f32 = jnp.float32
    dma = pltpu.SemaphoreType.DMA
    results = pl.pallas_call(
        functools.partial(kernel, sizes),
        out_shape=(jax.ShapeDtypeStruct((rows, columns), f32),) * 2,
        in_specs=[pl.BlockSpec(memory_space=pltpu.HBM)] * 7,
        out_specs=(vmem, vmem),
        scratch_shapes=[
            pltpu.VMEM(pair_src.shape, jnp.int32),
            pltpu.VMEM(pair_tgt.shape, jnp.int32),
            pltpu.VMEM(cross_slots.shape, jnp.int32),
            pltpu.VMEM((rows, columns), f32),
            pltpu.VMEM((1, rows), f32),
            pltpu.VMEM(table.shape, f32),
            pltpu.VMEM(blocks.shape, blocks.dtype),
            pltpu.VMEM((1, 128), f32),
            pltpu.VMEM((LINKS, 1, 128), f32),
            pltpu.VMEM((ITERS, PAIRS_IN, 1, columns), f32),
            pltpu.VMEM((ITERS, LINKS, 1, columns), f32),
            pltpu.VMEM((ITERS, PAIRS_IN, 4, columns), f32),
            pltpu.VMEM((ITERS, LINKS, 4, columns), f32),
            pltpu.VMEM((ITERS, 1, columns), f32),
            pltpu.VMEM((ITERS, 1, columns), f32),
            pltpu.VMEM((128, 128), f32),
            pltpu.VMEM((128, 128), f32),
            pltpu.VMEM((2, 3, 1, 128), f32),
            pltpu.VMEM((2, max(peers[0], 1), 1, 128), f32),
            pltpu.VMEM((2, max(peers[1], 1), 1, 128), f32),
            pltpu.VMEM((2, max(peers[2], 1), 1, 128), f32),
            dma((6,)),
            dma((2,)),
            pltpu.SemaphoreType.REGULAR((4,)),
            dma((LINKS,)),
            dma((LINKS,)),
            dma((2 * ITERS, LINKS)),
            dma((2 * ITERS, LINKS)),
            dma((ITERS,)),
            dma((ITERS,)),
            dma((2, sum(peers))),
            dma((2, sum(peers))),
        ],
        compiler_params=pltpu.CompilerParams(collective_id=0, has_side_effects=True),
    )(
        pair_src,
        pair_tgt,
        cross_slots,
        positions,
        stiffness.reshape(1, rows),
        jnp.asarray(table),
        blocks,
    )
    return pl.pallas_call(
        hand_over,
        out_shape=(jax.ShapeDtypeStruct((rows, columns), f32),) * 2,
        in_specs=[vmem, vmem],
        out_specs=(vmem, vmem),
    )(*results)


def program(split):
    sizes = tuple(split.shape[name] for name in SECTOR_RADIAL)
    placed = (
        P(SECTOR_RADIAL, None),
        P(SECTOR_RADIAL),
        P(None, SECTOR_RADIAL, None, None),
        P(None, SECTOR_RADIAL),
        P(None, SECTOR_RADIAL),
        P(SECTOR_RADIAL, None),
    )
    return jax.shard_map(
        functools.partial(local, sizes, bending_table(256)),
        mesh=split,
        in_specs=placed,
        out_specs=(P(SECTOR_RADIAL, None), P(SECTOR_RADIAL, None)),
        check_vma=False,
    )


def solution(mesh):
    split = Mesh(mesh.devices.reshape(4, 16, 2, 2, mesh.shape["radial"]), SECTOR_RADIAL)
    return program(split)
```

```python
import functools

import jax
import jax.numpy as jnp
import numpy as np
from jax import lax
from jax.experimental import pallas as pl
from jax.experimental.pallas import tpu as pltpu
from jax.sharding import Mesh
from jax.sharding import PartitionSpec as P

ITERS = 3
SECTOR = ("sector_0", "sector_1", "sector_2", "sector_3")
SECTOR_RADIAL = ("sector_0", "sector_1", "sector_2", "sector_3", "radial")
MESH = pl.DeviceIdType.MESH
EPSILON = 1e-06
GAMMA = 64.0
PAIRS_IN = 3
LINKS = 5


def bending_table(points):
    k = np.arange(points)
    weights = (np.minimum(k, points - k) / (points // 2)) ** 4 / points
    angles = (k[:, None] * k[None, :] % points) * (2.0 * np.pi / points)
    table = (np.cos(angles) * weights) @ np.cos(angles).T + (np.sin(angles) * weights) @ np.sin(angles).T
    return table.astype(np.float32)


def dot_nt(a, b, precision=None):
    return lax.dot_general(
        a, b, (((1,), (1,)), ((), ())), preferred_element_type=jnp.float32, precision=precision
    )


def total_of(terms):
    terms = list(terms)
    return functools.reduce(lambda a, b: a + b, terms)


def krylov_weights(gram):
    at = lambda i, j: gram[(min(i, j), max(i, j))]
    first = jnp.sqrt(at(0, 0) + EPSILON)
    basis = [[1.0 / first]]
    hess = {}
    for j in range(ITERS):
        image = [GAMMA * a for a in basis[j]]
        seen = [total_of(at(i, m + 1) * image[m] for m in range(j + 1)) for i in range(j + 1)]
        h = [total_of(basis[i][a] * seen[a] for a in range(i + 1)) for i in range(j + 1)]
        left = []
        for a in range(j + 2):
            value = image[a - 1] if a > 0 else None
            for i in range(a, j + 1):
                term = h[i] * basis[i][a]
                value = -term if value is None else value - term
            left.append(value)
        square = total_of(
            left[a] * total_of(at(a, b) * left[b] for b in range(j + 2)) for a in range(j + 2)
        )
        norm = jnp.sqrt(jnp.maximum(square, 0.0) + EPSILON)
        for i in range(j + 1):
            hess[(i, j)] = h[i]
        hess[(j + 1, j)] = norm
        scale = 1.0 / norm
        basis.append([a * scale for a in left])
    normal = {}
    for i in range(ITERS):
        for j in range(i + 1):
            normal[(i, j)] = total_of(hess[(k, i)] * hess[(k, j)] for k in range(min(i, j) + 2))
    moment = [first * hess[(0, j)] for j in range(ITERS)]
    factor, inverse = {}, []
    for i in range(ITERS):
        for j in range(i):
            value = normal[(i, j)]
            for k in range(j):
                value = value - factor[(i, k)] * factor[(j, k)]
            factor[(i, j)] = value * inverse[j]
        value = normal[(i, i)]
        for k in range(i):
            value = value - factor[(i, k)] * factor[(i, k)]
        inverse.append(1.0 / jnp.sqrt(value))
    forward = []
    for i in range(ITERS):
        value = moment[i]
        for k in range(i):
            value = value - factor[(i, k)] * forward[k]
        forward.append(value * inverse[i])
    coefficients = [None] * ITERS
    for i in reversed(range(ITERS)):
        value = forward[i]
        for k in range(i + 1, ITERS):
            value = value - factor[(k, i)] * coefficients[k]
        coefficients[i] = value * inverse[i]
    return [
        total_of(coefficients[j] * basis[j][a] for j in range(a, ITERS)) for a in range(ITERS)
    ]


def kernel(
    sizes,
    src_any,
    tgt_any,
    slot_any,
    pos_any,
    stiff_any,
    fourth_any,
    blocks_ref,
    after_ref,
    final_ref,
    src_ref,
    tgt_ref,
    slot_ref,
    pos_ref,
    stiff_ref,
    fourth_ref,
    block_buf,
    id_out,
    id_in,
    near_out,
    near_in,
    wide_out,
    wide_in,
    row_out,
    row_in,
    gram_buf,
    scalar_buf,
    sum_out,
    sum_in_0,
    sum_in_1,
    load_sem,
    block_sem,
    ready_sem,
    id_send,
    id_recv,
    near_send,
    near_recv,
    row_send,
    row_recv,
    sum_send,
    sum_recv,
):
    ny, nz, nx, nc, nr = sizes
    rows, columns = pos_ref.shape
    points = columns // 2
    y, z, x, c, r = (lax.axis_index(name) for name in SECTOR_RADIAL)
    sectors = ny * nz * nx * nc
    sector = ((y * nz + z) * nx + x) * nc + c
    own_base = (sector * nr + r) * rows

    def place(index, radial):
        return (
            lax.div(index, nc * nx * nz),
            lax.rem(lax.div(index, nc * nx), nz),
            lax.rem(lax.div(index, nc), nx),
            lax.rem(index, nc),
            radial,
        )

    before = lax.rem(sector + sectors - 1, sectors)
    after = lax.rem(sector + 1, sectors)
    other = lax.rem(r + 1, nr)
    links = [
        (0, place(before, r)),
        (0, place(before, other)),
        (1, (y, z, x, c, other)),
        (2, place(after, r)),
        (2, place(after, other)),
    ]

    stage_0 = [
        (lax.rem(x + i, nx), lax.rem(c + j, nc), lax.rem(r + k, nr))
        for i in range(nx)
        for j in range(nc)
        for k in range(nr)
    ]
    stages = [
        [
            (lax.rem(y + i, ny), z, a, b, d)
            for i in range(ny)
            for n, (a, b, d) in enumerate(stage_0)
            if i or n
        ],
        [(y, lax.rem(z + i, nz), x, c, r) for i in range(1, nz)],
    ]
    columns_y = [(lax.rem(y + i, ny), z, x, c, r) for i in range(1, ny)]

    def around(distance):
        steps = sorted({distance % nz, -distance % nz} - {0})
        return [(y, lax.rem(z + step, nz), x, c, r) for step in steps]

    barrier = pltpu.get_barrier_semaphore()
    greeted = [device for _, device in links] + stages[0][: nx * nc * nr - 1] + columns_y + around(1)
    for device in greeted:
        pl.semaphore_signal(barrier, inc=1, device_id=device, device_id_type=MESH)

    small = [
        pltpu.make_async_copy(source, target, load_sem.at[n])
        for n, (source, target) in enumerate(
            (
                (src_any, src_ref),
                (tgt_any, tgt_ref),
                (slot_any, slot_ref),
                (stiff_any, stiff_ref),
                (pos_any, pos_ref),
                (fourth_any, fourth_ref),
            )
        )
    ]
    loads = [
        pltpu.make_async_copy(blocks_ref.at[k], block_buf.at[k], block_sem.at[k]) for k in range(2)
    ]
    for load in small + loads:
        load.start()

    reach = [1]
    while 2 * reach[-1] < nz:
        reach.append(2 * reach[-1])
    reach = reach[:-1] if len(reach) > 1 else []

    def tell(n):
        for device in around(reach[n]):
            pl.semaphore_signal(
                ready_sem.at[n], inc=1, device_id=device, device_id_type=MESH
            )

    def hear(n):
        pl.semaphore_wait(ready_sem.at[n], len(around(reach[n])))

    for load in small:
        load.wait()

    lane = lax.broadcasted_iota(jnp.int32, (1, 128), 1)
    row_of = lax.broadcasted_iota(jnp.int32, (rows, 1), 0)
    row_wide = lax.broadcasted_iota(jnp.int32, (rows, columns), 0)
    eye = lax.broadcasted_iota(jnp.int32, (rows, rows), 0) == lax.broadcasted_iota(
        jnp.int32, (rows, rows), 1
    )
    stiff_row = stiff_ref[...]
    stiff = jnp.sum(jnp.where(eye, stiff_row, 0.0), axis=1, keepdims=True)
    slot = slot_ref[...]
    leaving_stiff = jnp.sum(jnp.where(row_of == slot, stiff, 0.0), axis=0, keepdims=True)

    pair_at = [lax.broadcasted_iota(jnp.int32, (2, PAIRS_IN), axis) for axis in range(2)]

    def entry(ref, k, p):
        chosen = (pair_at[0] == k) & (pair_at[1] == p)
        row = jnp.sum(jnp.where(chosen, ref[...].astype(jnp.float32), 0.0), axis=1, keepdims=True)
        return jnp.sum(row, axis=0, keepdims=True)

    targets = {(k, p): entry(tgt_ref, k, p) for k in range(2) for p in range(PAIRS_IN)}
    sources = {
        (k, p): entry(src_ref, k, p).astype(jnp.int32) - own_base
        for k in range(2)
        for p in range(PAIRS_IN)
    }
    ids = jnp.where(lane == 6, leaving_stiff, 0.0)
    for k in range(2):
        for p in range(PAIRS_IN):
            ids = jnp.where(lane == k * PAIRS_IN + p, targets[k, p], ids)
    id_out[...] = ids

    def send(source, target, send_sem, recv_sem, device):
        copy = pltpu.make_async_remote_copy(
            src_ref=source,
            dst_ref=target,
            send_sem=send_sem,
            recv_sem=recv_sem,
            device_id=device,
            device_id_type=MESH,
        )
        copy.start()
        return copy

    sent = []
    def targets_of(k):
        masks = []
        for l, (pair, _) in enumerate(links):
            target = jnp.sum(
                jnp.where(lane == k * PAIRS_IN + pair, id_in[l], 0.0), axis=1, keepdims=True
            )
            masks.append(row_of == target.astype(jnp.int32) - own_base)
        masks.append(row_of == targets[k, 1].astype(jnp.int32) - own_base)
        return [mask.astype(jnp.float32) for mask in masks]

    fourth = fourth_ref[...]
    operand_row = lax.broadcasted_iota(jnp.int32, (8, columns), 0)

    def product_of(fields, k, p):
        mask = row_wide == sources[k, p]
        stacked = jnp.zeros((8, columns), jnp.float32)
        for j, field in enumerate(fields):
            picked = jnp.sum(jnp.where(mask, field, 0.0), axis=0, keepdims=True)
            stacked = jnp.where(lax.rem(operand_row, 4) == j, picked, stacked)
        high = stacked.astype(jnp.bfloat16).astype(jnp.float32)
        operand = jnp.where(operand_row < 4, high, stacked - high).astype(jnp.bfloat16)
        product = dot_nt(operand, block_buf[k, p])
        product = product[0:4] + product[4:8]
        return product[0:1] if len(fields) == 1 else product

    def ends_of(exchange):
        if exchange >= ITERS:
            return wide_out.at[exchange - ITERS], wide_in.at[exchange - ITERS]
        return near_out.at[exchange], near_in.at[exchange]

    def launch(exchange, p):
        source, target = ends_of(exchange)
        copies = {
            l: send(
                source.at[pair],
                target.at[l],
                near_send.at[exchange, l],
                near_recv.at[exchange, l],
                device,
            )
            for l, (pair, device) in enumerate(links)
            if pair == p
        }
        sent.extend(copies.values())
        return copies

    def dispatch(fields, k, exchange):
        copies = {}
        for p in (0, 2, 1):
            own = product_of(fields, k, p)
            ends_of(exchange)[0][p] = own
            copies.update(launch(exchange, p))
        return own, copies

    def bend(fields, bending):
        halves = [f[:, i * points : (i + 1) * points] for f in fields for i in range(2)]
        curved = jnp.dot(
            jnp.concatenate(halves, axis=0),
            fourth,
            preferred_element_type=jnp.float32,
            precision=lax.Precision.HIGHEST,
        )
        images = []
        for j, field in enumerate(fields):
            x_part = curved[2 * j * rows : (2 * j + 1) * rows]
            y_part = curved[(2 * j + 1) * rows : (2 * j + 2) * rows]
            images.append(field + bending * jnp.concatenate([x_part, y_part], axis=1))
        return images

    def receive(images, own, copies, exchange, masks):
        wide = exchange >= ITERS
        images = [image + masks[LINKS] * own[j : j + 1] for j, image in enumerate(images)]
        for l in sorted(copies):
            copies[l].wait_recv()
            arrived = wide_in[exchange - ITERS, l] if wide else near_in[exchange, l]
            images = [
                image + masks[l] * arrived[j : j + 1] for j, image in enumerate(images)
            ]
        return [image * (1.0 / GAMMA) for image in images]

    def folded(product):
        wide = total_of(product[:, i * 128 : (i + 1) * 128] for i in range(columns // 128))
        return jnp.sum(wide, axis=0, keepdims=True)

    gram_pairs = [(i, j) for i in range(ITERS + 1) for j in range(i, ITERS + 1)]

    def gram_sums(basis):
        for n, (i, j) in enumerate(gram_pairs):
            gram_buf[n : n + 1, :] = folded(basis[i] * basis[j])
        sums = dot_nt(jnp.ones((8, 128), jnp.float32), gram_buf[...], lax.Precision.HIGHEST)
        return sums[0:1]

    order = [1, 0]
    inboxes = (sum_in_0, sum_in_1)

    def stage_start(values, which, t):
        stage, inbox = stages[t], inboxes[t]
        first = sum(len(s) for s in stages[:t])
        sum_out[which, t] = values
        copies = [
            send(
                sum_out.at[which, t],
                inbox.at[which, i],
                sum_send.at[which, first + i],
                sum_recv.at[which, first + i],
                device,
            )
            for i, device in enumerate(stage)
        ]
        sent.extend(copies)
        return copies

    def stage_end(values, copies, which, t):
        for i, copy in enumerate(copies):
            copy.wait_recv()
            values = values + inboxes[t][which, i]
        return values

    def weights_of(values):
        diagonal = lax.broadcasted_iota(jnp.int32, (128, 128), 0) == lax.broadcasted_iota(
            jnp.int32, (128, 128), 1
        )
        scalar_buf[...] = jnp.dot(
            jnp.where(diagonal, values, 0.0),
            jnp.ones((128, 128), jnp.float32),
            preferred_element_type=jnp.float32,
            precision=lax.Precision.HIGHEST,
        )
        weights = krylov_weights(
            {pair: scalar_buf[n : n + 1, :] for n, pair in enumerate(gram_pairs)}
        )
        return [jnp.broadcast_to(weight[:, 0:1], (rows, columns)) for weight in weights]

    def cross(field, j):
        row_out[j] = jnp.sum(jnp.where(row_wide == slot, field, 0.0), axis=0, keepdims=True)
        copy = send(row_out.at[j], row_in.at[j], row_send.at[j], row_recv.at[j], links[3][1])
        sent.append(copy)
        return copy

    gram_buf[...] = jnp.zeros_like(gram_buf)
    start = pos_ref[...]
    loads[0].wait()
    for p in (0, 2, 1):
        own = product_of([start], 0, p)
        near_out[0, p] = own
    images = bend([start], stiff)

    pl.semaphore_wait(barrier, len(greeted))
    copies = {l: copy for p in (0, 2, 1) for l, copy in launch(0, p).items()}
    id_copies = [
        send(id_out, id_in.at[l], id_send.at[l], id_recv.at[l], device)
        for l, (_, device) in enumerate(links)
    ]
    sent += id_copies
    if reach:
        tell(0)
    for device in columns_y:
        pl.semaphore_signal(ready_sem.at[3], inc=1, device_id=device, device_id_type=MESH)
    crossings = [cross(start, 0)]
    loads[1].wait()
    for copy in id_copies:
        copy.wait_recv()
    masks = targets_of(0)
    later_masks = targets_of(1)
    new_stiff = jnp.sum(jnp.where(lane == 6, id_in[3], 0.0), axis=1, keepdims=True)
    moved_stiff = jnp.where(row_of == slot, new_stiff, stiff)

    basis = [start] + receive(images, own, copies, 0, masks)
    for j in range(1, ITERS):
        own, copies = dispatch([basis[j]], 0, j)
        crossings.append(cross(basis[j], j))
        if j - 1 < len(reach):
            hear(j - 1)
            if j < len(reach):
                tell(j)
        images = bend([basis[j]], stiff)
        basis += receive(images, own, copies, j, masks)

    if columns_y:
        pl.semaphore_wait(ready_sem.at[3], len(columns_y))
    for n in range(ITERS - 1, len(reach)):
        hear(n)
        if n + 1 < len(reach):
            tell(n + 1)
    level = []
    for j in range(ITERS):
        crossings[j].wait_recv()
        level.append(jnp.where(row_wide == slot, row_in[j], basis[j]))
    levels = [level]
    flying = None
    for j in range(ITERS):
        exchange = ITERS + j
        own, copies = dispatch(levels[j], 1, exchange)
        if j == 0:
            values = gram_sums(basis)
        elif j <= len(order):
            values = stage_end(values, flying, 0, order[j - 1])
        if j < len(order):
            flying = stage_start(values, 0, order[j])
        elif j == len(order):
            weights = weights_of(values)
        images = bend(levels[j], moved_stiff)
        levels.append(receive(images, own, copies, exchange, later_masks))
    second = [total_of(w * part for w, part in zip(weights, parts)) for parts in levels]
    after_ref[...] = second[0]
    values = gram_sums(second)
    done = list(sent)
    for t in order:
        flying = stage_start(values, 1, t)
        if t == order[0]:
            for copy in done:
                copy.wait_send()
        values = stage_end(values, flying, 1, t)
    weights = weights_of(values)
    final_ref[...] = total_of(w * part for w, part in zip(weights, second))
    for copy in sent[len(done) :]:
        copy.wait_send()


def hand_over(after_in, final_in, after_ref, final_ref):
    after_ref[...] = after_in[...]
    final_ref[...] = final_in[...]


def local(sizes, table, positions, stiffness, blocks, pair_src, pair_tgt, cross_slots):
    rows, columns = positions.shape
    ny, nz, nx, nc, nr = sizes
    peers = (ny * nx * nc * nr - 1, nz - 1)
    vmem = pl.BlockSpec(memory_space=pltpu.VMEM)
    f32 = jnp.float32
    dma = pltpu.SemaphoreType.DMA
    results = pl.pallas_call(
        functools.partial(kernel, sizes),
        out_shape=(jax.ShapeDtypeStruct((rows, columns), f32),) * 2,
        in_specs=[pl.BlockSpec(memory_space=pltpu.HBM)] * 7,
        out_specs=(vmem, vmem),
        scratch_shapes=[
            pltpu.VMEM(pair_src.shape, jnp.int32),
            pltpu.VMEM(pair_tgt.shape, jnp.int32),
            pltpu.VMEM(cross_slots.shape, jnp.int32),
            pltpu.VMEM((rows, columns), f32),
            pltpu.VMEM((1, rows), f32),
            pltpu.VMEM(table.shape, f32),
            pltpu.VMEM(blocks.shape, blocks.dtype),
            pltpu.VMEM((1, 128), f32),
            pltpu.VMEM((LINKS, 1, 128), f32),
            pltpu.VMEM((ITERS, PAIRS_IN, 1, columns), f32),
            pltpu.VMEM((ITERS, LINKS, 1, columns), f32),
            pltpu.VMEM((ITERS, PAIRS_IN, 4, columns), f32),
            pltpu.VMEM((ITERS, LINKS, 4, columns), f32),
            pltpu.VMEM((ITERS, 1, columns), f32),
            pltpu.VMEM((ITERS, 1, columns), f32),
            pltpu.VMEM((128, 128), f32),
            pltpu.VMEM((128, 128), f32),
            pltpu.VMEM((2, 2, 1, 128), f32),
            pltpu.VMEM((2, max(peers[0], 1), 1, 128), f32),
            pltpu.VMEM((2, max(peers[1], 1), 1, 128), f32),
            dma((6,)),
            dma((2,)),
            pltpu.SemaphoreType.REGULAR((4,)),
            dma((LINKS,)),
            dma((LINKS,)),
            dma((2 * ITERS, LINKS)),
            dma((2 * ITERS, LINKS)),
            dma((ITERS,)),
            dma((ITERS,)),
            dma((2, sum(peers))),
            dma((2, sum(peers))),
        ],
        compiler_params=pltpu.CompilerParams(collective_id=0, has_side_effects=True),
    )(
        pair_src,
        pair_tgt,
        cross_slots,
        positions,
        stiffness.reshape(1, rows),
        jnp.asarray(table),
        blocks,
    )
    return pl.pallas_call(
        hand_over,
        out_shape=(jax.ShapeDtypeStruct((rows, columns), f32),) * 2,
        in_specs=[vmem, vmem],
        out_specs=(vmem, vmem),
    )(*results)


def program(split):
    sizes = tuple(split.shape[name] for name in SECTOR_RADIAL)
    placed = (
        P(SECTOR_RADIAL, None),
        P(SECTOR_RADIAL),
        P(None, SECTOR_RADIAL, None, None),
        P(None, SECTOR_RADIAL),
        P(None, SECTOR_RADIAL),
        P(SECTOR_RADIAL, None),
    )
    return jax.shard_map(
        functools.partial(local, sizes, bending_table(256)),
        mesh=split,
        in_specs=placed,
        out_specs=(P(SECTOR_RADIAL, None), P(SECTOR_RADIAL, None)),
        check_vma=False,
    )


def solution(mesh):
    split = Mesh(mesh.devices.reshape(4, 16, 2, 2, mesh.shape["radial"]), SECTOR_RADIAL)
    return program(split)
```

```python
import functools

import jax
import jax.numpy as jnp
import numpy as np
from jax import lax
from jax.experimental import pallas as pl
from jax.experimental.pallas import tpu as pltpu
from jax.sharding import Mesh
from jax.sharding import PartitionSpec as P

ITERS = 3
SECTOR = ("sector_0", "sector_1", "sector_2", "sector_3")
SECTOR_RADIAL = ("sector_0", "sector_1", "sector_2", "sector_3", "radial")
MESH = pl.DeviceIdType.MESH
EPSILON = 1e-06
GAMMA = 64.0
PAIRS_IN = 3
LINKS = 5


def bending_table(points):
    k = np.arange(points)
    weights = (np.minimum(k, points - k) / (points // 2)) ** 4 / points
    angles = (k[:, None] * k[None, :] % points) * (2.0 * np.pi / points)
    table = (np.cos(angles) * weights) @ np.cos(angles).T + (np.sin(angles) * weights) @ np.sin(angles).T
    return table.astype(np.float32)


def dot_nt(a, b, precision=None):
    return lax.dot_general(
        a, b, (((1,), (1,)), ((), ())), preferred_element_type=jnp.float32, precision=precision
    )


def total_of(terms):
    terms = list(terms)
    return functools.reduce(lambda a, b: a + b, terms)


def krylov_weights(gram):
    at = lambda i, j: gram[(min(i, j), max(i, j))]
    first = jnp.sqrt(at(0, 0) + EPSILON)
    basis = [[1.0 / first]]
    hess = {}
    for j in range(ITERS):
        image = [GAMMA * a for a in basis[j]]
        seen = [total_of(at(i, m + 1) * image[m] for m in range(j + 1)) for i in range(j + 1)]
        h = [total_of(basis[i][a] * seen[a] for a in range(i + 1)) for i in range(j + 1)]
        left = []
        for a in range(j + 2):
            value = image[a - 1] if a > 0 else None
            for i in range(a, j + 1):
                term = h[i] * basis[i][a]
                value = -term if value is None else value - term
            left.append(value)
        square = total_of(
            left[a] * total_of(at(a, b) * left[b] for b in range(j + 2)) for a in range(j + 2)
        )
        norm = jnp.sqrt(jnp.maximum(square, 0.0) + EPSILON)
        for i in range(j + 1):
            hess[(i, j)] = h[i]
        hess[(j + 1, j)] = norm
        scale = 1.0 / norm
        basis.append([a * scale for a in left])
    normal = {}
    for i in range(ITERS):
        for j in range(i + 1):
            normal[(i, j)] = total_of(hess[(k, i)] * hess[(k, j)] for k in range(min(i, j) + 2))
    moment = [first * hess[(0, j)] for j in range(ITERS)]
    factor, inverse = {}, []
    for i in range(ITERS):
        for j in range(i):
            value = normal[(i, j)]
            for k in range(j):
                value = value - factor[(i, k)] * factor[(j, k)]
            factor[(i, j)] = value * inverse[j]
        value = normal[(i, i)]
        for k in range(i):
            value = value - factor[(i, k)] * factor[(i, k)]
        inverse.append(1.0 / jnp.sqrt(value))
    forward = []
    for i in range(ITERS):
        value = moment[i]
        for k in range(i):
            value = value - factor[(i, k)] * forward[k]
        forward.append(value * inverse[i])
    coefficients = [None] * ITERS
    for i in reversed(range(ITERS)):
        value = forward[i]
        for k in range(i + 1, ITERS):
            value = value - factor[(k, i)] * coefficients[k]
        coefficients[i] = value * inverse[i]
    return [
        total_of(coefficients[j] * basis[j][a] for j in range(a, ITERS)) for a in range(ITERS)
    ]


def kernel(
    sizes,
    src_any,
    tgt_any,
    slot_any,
    pos_any,
    stiff_any,
    fourth_any,
    blocks_ref,
    after_ref,
    final_ref,
    src_ref,
    tgt_ref,
    slot_ref,
    pos_ref,
    stiff_ref,
    fourth_ref,
    block_buf,
    id_out,
    id_in,
    near_out,
    near_in,
    wide_out,
    wide_in,
    row_out,
    row_in,
    gram_buf,
    scalar_buf,
    sum_out,
    sum_in_0,
    sum_in_1,
    load_sem,
    block_sem,
    ready_sem,
    id_send,
    id_recv,
    near_send,
    near_recv,
    row_send,
    row_recv,
    sum_send,
    sum_recv,
):
    ny, nz, nx, nc, nr = sizes
    rows, columns = pos_ref.shape
    points = columns // 2
    y, z, x, c, r = (lax.axis_index(name) for name in SECTOR_RADIAL)
    sectors = ny * nz * nx * nc
    sector = ((y * nz + z) * nx + x) * nc + c
    own_base = (sector * nr + r) * rows

    def place(index, radial):
        return (
            lax.div(index, nc * nx * nz),
            lax.rem(lax.div(index, nc * nx), nz),
            lax.rem(lax.div(index, nc), nx),
            lax.rem(index, nc),
            radial,
        )

    before = lax.rem(sector + sectors - 1, sectors)
    after = lax.rem(sector + 1, sectors)
    other = lax.rem(r + 1, nr)
    links = [
        (0, place(before, r)),
        (0, place(before, other)),
        (1, (y, z, x, c, other)),
        (2, place(after, r)),
        (2, place(after, other)),
    ]

    def ring(step, size):
        return min(step, size - step)

    plane = sorted(
        (
            (-ring(i, ny) - (a if a else 2 * k), i, a, b, k)
            for i in range(ny)
            for a in range(nx)
            for b in range(nc)
            for k in range(nr)
            if i or a or b or k
        ),
    )
    at_plane = lambda i, a, b, k: (
        lax.rem(y + i, ny),
        z,
        lax.rem(x + a, nx),
        lax.rem(c + b, nc),
        lax.rem(r + k, nr),
    )
    beside = [at_plane(*step) for _, *step in plane if step[0] == 0]
    far_z = sorted(range(1, nz), key=lambda step: -ring(step, nz))
    stages = [
        [at_plane(*step) for _, *step in plane],
        [(y, lax.rem(z + step, nz), x, c, r) for step in far_z],
    ]
    columns_y = [(lax.rem(y + i, ny), z, x, c, r) for i in range(1, ny)]

    def around(distance):
        steps = sorted({distance % nz, -distance % nz} - {0})
        return [(y, lax.rem(z + step, nz), x, c, r) for step in steps]

    barrier = pltpu.get_barrier_semaphore()
    greeted = [device for _, device in links] + beside + columns_y + around(1)
    for device in greeted:
        pl.semaphore_signal(barrier, inc=1, device_id=device, device_id_type=MESH)

    small = [
        pltpu.make_async_copy(source, target, load_sem.at[n])
        for n, (source, target) in enumerate(
            (
                (src_any, src_ref),
                (tgt_any, tgt_ref),
                (slot_any, slot_ref),
                (stiff_any, stiff_ref),
                (pos_any, pos_ref),
                (fourth_any, fourth_ref),
            )
        )
    ]
    loads = [
        pltpu.make_async_copy(blocks_ref.at[k], block_buf.at[k], block_sem.at[k]) for k in range(2)
    ]
    for load in small + loads:
        load.start()

    reach = [1]
    while 2 * reach[-1] < nz:
        reach.append(2 * reach[-1])
    reach = reach[:-1] if len(reach) > 1 else []

    def tell(n):
        for device in around(reach[n]):
            pl.semaphore_signal(
                ready_sem.at[n], inc=1, device_id=device, device_id_type=MESH
            )

    def hear(n):
        pl.semaphore_wait(ready_sem.at[n], len(around(reach[n])))

    for load in small:
        load.wait()

    lane = lax.broadcasted_iota(jnp.int32, (1, 128), 1)
    row_of = lax.broadcasted_iota(jnp.int32, (rows, 1), 0)
    row_wide = lax.broadcasted_iota(jnp.int32, (rows, columns), 0)
    eye = lax.broadcasted_iota(jnp.int32, (rows, rows), 0) == lax.broadcasted_iota(
        jnp.int32, (rows, rows), 1
    )
    stiff_row = stiff_ref[...]
    stiff = jnp.sum(jnp.where(eye, stiff_row, 0.0), axis=1, keepdims=True)
    slot = slot_ref[...]
    leaving_stiff = jnp.sum(jnp.where(row_of == slot, stiff, 0.0), axis=0, keepdims=True)

    pair_at = [lax.broadcasted_iota(jnp.int32, (2, PAIRS_IN), axis) for axis in range(2)]

    def entry(ref, k, p):
        chosen = (pair_at[0] == k) & (pair_at[1] == p)
        row = jnp.sum(jnp.where(chosen, ref[...].astype(jnp.float32), 0.0), axis=1, keepdims=True)
        return jnp.sum(row, axis=0, keepdims=True)

    targets = {(k, p): entry(tgt_ref, k, p) for k in range(2) for p in range(PAIRS_IN)}
    sources = {
        (k, p): entry(src_ref, k, p).astype(jnp.int32) - own_base
        for k in range(2)
        for p in range(PAIRS_IN)
    }
    ids = jnp.where(lane == 6, leaving_stiff, 0.0)
    for k in range(2):
        for p in range(PAIRS_IN):
            ids = jnp.where(lane == k * PAIRS_IN + p, targets[k, p], ids)
    id_out[...] = ids

    def send(source, target, send_sem, recv_sem, device):
        copy = pltpu.make_async_remote_copy(
            src_ref=source,
            dst_ref=target,
            send_sem=send_sem,
            recv_sem=recv_sem,
            device_id=device,
            device_id_type=MESH,
        )
        copy.start()
        return copy

    sent = []
    def targets_of(k):
        masks = []
        for l, (pair, _) in enumerate(links):
            target = jnp.sum(
                jnp.where(lane == k * PAIRS_IN + pair, id_in[l], 0.0), axis=1, keepdims=True
            )
            masks.append(row_of == target.astype(jnp.int32) - own_base)
        masks.append(row_of == targets[k, 1].astype(jnp.int32) - own_base)
        return [mask.astype(jnp.float32) for mask in masks]

    fourth = fourth_ref[...]
    operand_row = lax.broadcasted_iota(jnp.int32, (8, columns), 0)

    def product_of(fields, k, p):
        mask = row_wide == sources[k, p]
        stacked = jnp.zeros((8, columns), jnp.float32)
        for j, field in enumerate(fields):
            picked = jnp.sum(jnp.where(mask, field, 0.0), axis=0, keepdims=True)
            stacked = jnp.where(lax.rem(operand_row, 4) == j, picked, stacked)
        high = stacked.astype(jnp.bfloat16).astype(jnp.float32)
        operand = jnp.where(operand_row < 4, high, stacked - high).astype(jnp.bfloat16)
        product = dot_nt(operand, block_buf[k, p])
        product = product[0:4] + product[4:8]
        return product[0:1] if len(fields) == 1 else product

    def ends_of(exchange):
        if exchange >= ITERS:
            return wide_out.at[exchange - ITERS], wide_in.at[exchange - ITERS]
        return near_out.at[exchange], near_in.at[exchange]

    def launch(exchange, p):
        source, target = ends_of(exchange)
        copies = {
            l: send(
                source.at[pair],
                target.at[l],
                near_send.at[exchange, l],
                near_recv.at[exchange, l],
                device,
            )
            for l, (pair, device) in enumerate(links)
            if pair == p
        }
        sent.extend(copies.values())
        return copies

    def dispatch(fields, k, exchange):
        copies = {}
        for p in (0, 2, 1):
            own = product_of(fields, k, p)
            ends_of(exchange)[0][p] = own
            copies.update(launch(exchange, p))
        return own, copies

    def bend(fields, bending):
        halves = [f[:, i * points : (i + 1) * points] for f in fields for i in range(2)]
        curved = jnp.dot(
            jnp.concatenate(halves, axis=0),
            fourth,
            preferred_element_type=jnp.float32,
            precision=lax.Precision.HIGHEST,
        )
        images = []
        for j, field in enumerate(fields):
            x_part = curved[2 * j * rows : (2 * j + 1) * rows]
            y_part = curved[(2 * j + 1) * rows : (2 * j + 2) * rows]
            images.append(field + bending * jnp.concatenate([x_part, y_part], axis=1))
        return images

    def receive(images, own, copies, exchange, masks):
        wide = exchange >= ITERS
        images = [image + masks[LINKS] * own[j : j + 1] for j, image in enumerate(images)]
        for l in sorted(copies):
            copies[l].wait_recv()
            arrived = wide_in[exchange - ITERS, l] if wide else near_in[exchange, l]
            images = [
                image + masks[l] * arrived[j : j + 1] for j, image in enumerate(images)
            ]
        return [image * (1.0 / GAMMA) for image in images]

    def folded(product):
        wide = total_of(product[:, i * 128 : (i + 1) * 128] for i in range(columns // 128))
        return jnp.sum(wide, axis=0, keepdims=True)

    gram_pairs = [(i, j) for i in range(ITERS + 1) for j in range(i, ITERS + 1)]

    diagonal = lax.broadcasted_iota(jnp.int32, (16, 128), 0) == lax.broadcasted_iota(
        jnp.int32, (16, 128), 1
    )

    def gram_sums(basis):
        for n, (i, j) in enumerate(gram_pairs):
            gram_buf[n : n + 1, :] = folded(basis[i] * basis[j])
        sums = jnp.sum(gram_buf[...], axis=1, keepdims=True)
        return jnp.sum(jnp.where(diagonal, sums, 0.0), axis=0, keepdims=True)

    order = [1, 0]
    inboxes = (sum_in_0, sum_in_1)

    def stage_start(values, which, t):
        stage, inbox = stages[t], inboxes[t]
        first = sum(len(s) for s in stages[:t])
        sum_out[which, t] = values
        copies = [
            send(
                sum_out.at[which, t],
                inbox.at[which, i],
                sum_send.at[which, first + i],
                sum_recv.at[which, first + i],
                device,
            )
            for i, device in enumerate(stage)
        ]
        sent.extend(copies)
        return copies

    def stage_end(values, copies, which, t):
        for i, copy in enumerate(copies):
            copy.wait_recv()
            values = values + inboxes[t][which, i]
        return values

    def weights_of(values):
        spread = jnp.sum(jnp.where(diagonal, values, 0.0), axis=1, keepdims=True)
        scalar_buf[...] = jnp.broadcast_to(spread, scalar_buf.shape)
        weights = krylov_weights(
            {pair: scalar_buf[n : n + 1, :] for n, pair in enumerate(gram_pairs)}
        )
        return [jnp.broadcast_to(weight[:, 0:1], (rows, columns)) for weight in weights]

    def cross(field, j):
        row_out[j] = jnp.sum(jnp.where(row_wide == slot, field, 0.0), axis=0, keepdims=True)
        copy = send(row_out.at[j], row_in.at[j], row_send.at[j], row_recv.at[j], links[3][1])
        sent.append(copy)
        return copy

    gram_buf[...] = jnp.zeros_like(gram_buf)
    start = pos_ref[...]
    loads[0].wait()
    for p in (0, 2, 1):
        own = product_of([start], 0, p)
        near_out[0, p] = own
    images = bend([start], stiff)

    pl.semaphore_wait(barrier, len(greeted))
    copies = {l: copy for p in (0, 2, 1) for l, copy in launch(0, p).items()}
    id_copies = [
        send(id_out, id_in.at[l], id_send.at[l], id_recv.at[l], device)
        for l, (_, device) in enumerate(links)
    ]
    sent += id_copies
    if reach:
        tell(0)
    for device in columns_y:
        pl.semaphore_signal(ready_sem.at[3], inc=1, device_id=device, device_id_type=MESH)
    crossings = [cross(start, 0)]
    loads[1].wait()
    for copy in id_copies:
        copy.wait_recv()
    masks = targets_of(0)
    later_masks = targets_of(1)
    new_stiff = jnp.sum(jnp.where(lane == 6, id_in[3], 0.0), axis=1, keepdims=True)
    moved_stiff = jnp.where(row_of == slot, new_stiff, stiff)

    basis = [start] + receive(images, own, copies, 0, masks)
    for j in range(1, ITERS):
        own, copies = dispatch([basis[j]], 0, j)
        crossings.append(cross(basis[j], j))
        if j - 1 < len(reach):
            hear(j - 1)
            if j < len(reach):
                tell(j)
        images = bend([basis[j]], stiff)
        basis += receive(images, own, copies, j, masks)

    if columns_y:
        pl.semaphore_wait(ready_sem.at[3], len(columns_y))
    for n in range(ITERS - 1, len(reach)):
        hear(n)
        if n + 1 < len(reach):
            tell(n + 1)
    level = []
    for j in range(ITERS):
        crossings[j].wait_recv()
        level.append(jnp.where(row_wide == slot, row_in[j], basis[j]))
    levels = [level]
    flying = None
    for j in range(ITERS):
        exchange = ITERS + j
        own, copies = dispatch(levels[j], 1, exchange)
        if j == 0:
            values = gram_sums(basis)
        elif j <= len(order):
            values = stage_end(values, flying, 0, order[j - 1])
        if j < len(order):
            flying = stage_start(values, 0, order[j])
        elif j == len(order):
            weights = weights_of(values)
        images = bend(levels[j], moved_stiff)
        levels.append(receive(images, own, copies, exchange, later_masks))
    second = [total_of(w * part for w, part in zip(weights, parts)) for parts in levels]
    after_ref[...] = second[0]
    values = gram_sums(second)
    done = list(sent)
    for t in order:
        flying = stage_start(values, 1, t)
        if t == order[0]:
            for copy in done:
                copy.wait_send()
        values = stage_end(values, flying, 1, t)
    weights = weights_of(values)
    final_ref[...] = total_of(w * part for w, part in zip(weights, second))
    for copy in sent[len(done) :]:
        copy.wait_send()


def hand_over(after_in, final_in, after_ref, final_ref):
    after_ref[...] = after_in[...]
    final_ref[...] = final_in[...]


def local(sizes, table, positions, stiffness, blocks, pair_src, pair_tgt, cross_slots):
    rows, columns = positions.shape
    ny, nz, nx, nc, nr = sizes
    peers = (ny * nx * nc * nr - 1, nz - 1)
    vmem = pl.BlockSpec(memory_space=pltpu.VMEM)
    f32 = jnp.float32
    dma = pltpu.SemaphoreType.DMA
    results = pl.pallas_call(
        functools.partial(kernel, sizes),
        out_shape=(jax.ShapeDtypeStruct((rows, columns), f32),) * 2,
        in_specs=[pl.BlockSpec(memory_space=pltpu.HBM)] * 7,
        out_specs=(vmem, vmem),
        scratch_shapes=[
            pltpu.VMEM(pair_src.shape, jnp.int32),
            pltpu.VMEM(pair_tgt.shape, jnp.int32),
            pltpu.VMEM(cross_slots.shape, jnp.int32),
            pltpu.VMEM((rows, columns), f32),
            pltpu.VMEM((1, rows), f32),
            pltpu.VMEM(table.shape, f32),
            pltpu.VMEM(blocks.shape, blocks.dtype),
            pltpu.VMEM((1, 128), f32),
            pltpu.VMEM((LINKS, 1, 128), f32),
            pltpu.VMEM((ITERS, PAIRS_IN, 1, columns), f32),
            pltpu.VMEM((ITERS, LINKS, 1, columns), f32),
            pltpu.VMEM((ITERS, PAIRS_IN, 4, columns), f32),
            pltpu.VMEM((ITERS, LINKS, 4, columns), f32),
            pltpu.VMEM((ITERS, 1, columns), f32),
            pltpu.VMEM((ITERS, 1, columns), f32),
            pltpu.VMEM((16, 128), f32),
            pltpu.VMEM((16, 128), f32),
            pltpu.VMEM((2, 2, 1, 128), f32),
            pltpu.VMEM((2, max(peers[0], 1), 1, 128), f32),
            pltpu.VMEM((2, max(peers[1], 1), 1, 128), f32),
            dma((6,)),
            dma((2,)),
            pltpu.SemaphoreType.REGULAR((4,)),
            dma((LINKS,)),
            dma((LINKS,)),
            dma((2 * ITERS, LINKS)),
            dma((2 * ITERS, LINKS)),
            dma((ITERS,)),
            dma((ITERS,)),
            dma((2, sum(peers))),
            dma((2, sum(peers))),
        ],
        compiler_params=pltpu.CompilerParams(collective_id=0, has_side_effects=True),
    )(
        pair_src,
        pair_tgt,
        cross_slots,
        positions,
        stiffness.reshape(1, rows),
        jnp.asarray(table),
        blocks,
    )
    return pl.pallas_call(
        hand_over,
        out_shape=(jax.ShapeDtypeStruct((rows, columns), f32),) * 2,
        in_specs=[vmem, vmem],
        out_specs=(vmem, vmem),
    )(*results)


def program(split):
    sizes = tuple(split.shape[name] for name in SECTOR_RADIAL)
    placed = (
        P(SECTOR_RADIAL, None),
        P(SECTOR_RADIAL),
        P(None, SECTOR_RADIAL, None, None),
        P(None, SECTOR_RADIAL),
        P(None, SECTOR_RADIAL),
        P(SECTOR_RADIAL, None),
    )
    return jax.shard_map(
        functools.partial(local, sizes, bending_table(256)),
        mesh=split,
        in_specs=placed,
        out_specs=(P(SECTOR_RADIAL, None), P(SECTOR_RADIAL, None)),
        check_vma=False,
    )


def solution(mesh):
    split = Mesh(mesh.devices.reshape(4, 16, 2, 2, mesh.shape["radial"]), SECTOR_RADIAL)
    return program(split)
```

```python
import functools

import jax
import jax.numpy as jnp
import numpy as np
from jax import lax
from jax.experimental import pallas as pl
from jax.experimental.pallas import tpu as pltpu
from jax.sharding import Mesh
from jax.sharding import PartitionSpec as P

ITERS = 3
SECTOR = ("sector_0", "sector_1", "sector_2", "sector_3")
SECTOR_RADIAL = ("sector_0", "sector_1", "sector_2", "sector_3", "radial")
MESH = pl.DeviceIdType.MESH
EPSILON = 1e-06
GAMMA = 64.0
PAIRS_IN = 3
LINKS = 5


def bending_table(points):
    k = np.arange(points)
    weights = (np.minimum(k, points - k) / (points // 2)) ** 4 / points
    angles = (k[:, None] * k[None, :] % points) * (2.0 * np.pi / points)
    table = (np.cos(angles) * weights) @ np.cos(angles).T + (np.sin(angles) * weights) @ np.sin(angles).T
    return table.astype(np.float32)


def dot_nt(a, b, precision=None):
    return lax.dot_general(
        a, b, (((1,), (1,)), ((), ())), preferred_element_type=jnp.float32, precision=precision
    )


def total_of(terms):
    terms = list(terms)
    return functools.reduce(lambda a, b: a + b, terms)


def krylov_weights(gram):
    at = lambda i, j: gram[(min(i, j), max(i, j))]
    first = jnp.sqrt(at(0, 0) + EPSILON)
    basis = [[1.0 / first]]
    hess = {}
    for j in range(ITERS):
        image = [GAMMA * a for a in basis[j]]
        seen = [total_of(at(i, m + 1) * image[m] for m in range(j + 1)) for i in range(j + 1)]
        h = [total_of(basis[i][a] * seen[a] for a in range(i + 1)) for i in range(j + 1)]
        left = []
        for a in range(j + 2):
            value = image[a - 1] if a > 0 else None
            for i in range(a, j + 1):
                term = h[i] * basis[i][a]
                value = -term if value is None else value - term
            left.append(value)
        square = total_of(
            left[a] * total_of(at(a, b) * left[b] for b in range(j + 2)) for a in range(j + 2)
        )
        norm = jnp.sqrt(jnp.maximum(square, 0.0) + EPSILON)
        for i in range(j + 1):
            hess[(i, j)] = h[i]
        hess[(j + 1, j)] = norm
        scale = 1.0 / norm
        basis.append([a * scale for a in left])
    normal = {}
    for i in range(ITERS):
        for j in range(i + 1):
            normal[(i, j)] = total_of(hess[(k, i)] * hess[(k, j)] for k in range(min(i, j) + 2))
    moment = [first * hess[(0, j)] for j in range(ITERS)]
    factor, inverse = {}, []
    for i in range(ITERS):
        for j in range(i):
            value = normal[(i, j)]
            for k in range(j):
                value = value - factor[(i, k)] * factor[(j, k)]
            factor[(i, j)] = value * inverse[j]
        value = normal[(i, i)]
        for k in range(i):
            value = value - factor[(i, k)] * factor[(i, k)]
        inverse.append(1.0 / jnp.sqrt(value))
    forward = []
    for i in range(ITERS):
        value = moment[i]
        for k in range(i):
            value = value - factor[(i, k)] * forward[k]
        forward.append(value * inverse[i])
    coefficients = [None] * ITERS
    for i in reversed(range(ITERS)):
        value = forward[i]
        for k in range(i + 1, ITERS):
            value = value - factor[(k, i)] * coefficients[k]
        coefficients[i] = value * inverse[i]
    return [
        total_of(coefficients[j] * basis[j][a] for j in range(a, ITERS)) for a in range(ITERS)
    ]


def kernel(
    sizes,
    src_any,
    tgt_any,
    slot_any,
    pos_any,
    stiff_any,
    fourth_any,
    blocks_ref,
    after_ref,
    final_ref,
    src_ref,
    tgt_ref,
    slot_ref,
    pos_ref,
    stiff_ref,
    fourth_ref,
    block_buf,
    id_out,
    id_in,
    near_out,
    near_in,
    wide_out,
    wide_in,
    row_out,
    row_in,
    gram_buf,
    scalar_buf,
    sum_out,
    sum_in_0,
    sum_in_1,
    load_sem,
    block_sem,
    ready_sem,
    id_send,
    id_recv,
    near_send,
    near_recv,
    row_send,
    row_recv,
    sum_send,
    sum_recv,
):
    ny, nz, nx, nc, nr = sizes
    rows, columns = pos_ref.shape
    points = columns // 2
    y, z, x, c, r = (lax.axis_index(name) for name in SECTOR_RADIAL)
    sectors = ny * nz * nx * nc
    sector = ((y * nz + z) * nx + x) * nc + c
    own_base = (sector * nr + r) * rows

    def place(index, radial):
        return (
            lax.div(index, nc * nx * nz),
            lax.rem(lax.div(index, nc * nx), nz),
            lax.rem(lax.div(index, nc), nx),
            lax.rem(index, nc),
            radial,
        )

    before = lax.rem(sector + sectors - 1, sectors)
    after = lax.rem(sector + 1, sectors)
    other = lax.rem(r + 1, nr)
    links = [
        (0, place(before, r)),
        (0, place(before, other)),
        (1, (y, z, x, c, other)),
        (2, place(after, r)),
        (2, place(after, other)),
    ]

    def ring(step, size):
        return min(step, size - step)

    plane = sorted(
        (
            (-ring(i, ny) - (a if a else 2 * k), i, a, b, k)
            for i in range(ny)
            for a in range(nx)
            for b in range(nc)
            for k in range(nr)
            if i or a or b or k
        ),
    )
    at_plane = lambda i, a, b, k: (
        lax.rem(y + i, ny),
        z,
        lax.rem(x + a, nx),
        lax.rem(c + b, nc),
        lax.rem(r + k, nr),
    )
    beside = [at_plane(*step) for _, *step in plane if step[0] == 0]
    far_z = sorted(range(1, nz), key=lambda step: -ring(step, nz))
    stages = [
        [at_plane(*step) for _, *step in plane],
        [(y, lax.rem(z + step, nz), x, c, r) for step in far_z],
    ]
    columns_y = [(lax.rem(y + i, ny), z, x, c, r) for i in range(1, ny)]

    def around(distance):
        steps = sorted({distance % nz, -distance % nz} - {0})
        return [(y, lax.rem(z + step, nz), x, c, r) for step in steps]

    barrier = pltpu.get_barrier_semaphore()
    greeted = [device for _, device in links] + beside + columns_y + around(1)
    for device in greeted:
        pl.semaphore_signal(barrier, inc=1, device_id=device, device_id_type=MESH)

    small = [
        pltpu.make_async_copy(source, target, load_sem.at[n])
        for n, (source, target) in enumerate(
            (
                (src_any, src_ref),
                (tgt_any, tgt_ref),
                (slot_any, slot_ref),
                (stiff_any, stiff_ref),
                (pos_any, pos_ref),
                (fourth_any, fourth_ref),
            )
        )
    ]
    loads = [
        pltpu.make_async_copy(blocks_ref.at[k], block_buf.at[k], block_sem.at[k]) for k in range(2)
    ]
    for load in small + loads:
        load.start()

    reach = [1]
    while 2 * reach[-1] < nz:
        reach.append(2 * reach[-1])
    reach = reach[:-1] if len(reach) > 1 else []

    def tell(n):
        for device in around(reach[n]):
            pl.semaphore_signal(
                ready_sem.at[n], inc=1, device_id=device, device_id_type=MESH
            )

    def hear(n):
        pl.semaphore_wait(ready_sem.at[n], len(around(reach[n])))

    for load in small:
        load.wait()

    lane = lax.broadcasted_iota(jnp.int32, (1, 128), 1)
    row_of = lax.broadcasted_iota(jnp.int32, (rows, 1), 0)
    row_wide = lax.broadcasted_iota(jnp.int32, (rows, columns), 0)
    eye = lax.broadcasted_iota(jnp.int32, (rows, rows), 0) == lax.broadcasted_iota(
        jnp.int32, (rows, rows), 1
    )
    stiff_row = stiff_ref[...]
    stiff = jnp.sum(jnp.where(eye, stiff_row, 0.0), axis=1, keepdims=True)
    slot = slot_ref[...]
    leaving_stiff = jnp.sum(jnp.where(row_of == slot, stiff, 0.0), axis=0, keepdims=True)

    pair_at = [lax.broadcasted_iota(jnp.int32, (2, PAIRS_IN), axis) for axis in range(2)]

    def entry(ref, k, p):
        chosen = (pair_at[0] == k) & (pair_at[1] == p)
        row = jnp.sum(jnp.where(chosen, ref[...].astype(jnp.float32), 0.0), axis=1, keepdims=True)
        return jnp.sum(row, axis=0, keepdims=True)

    targets = {(k, p): entry(tgt_ref, k, p) for k in range(2) for p in range(PAIRS_IN)}
    sources = {
        (k, p): entry(src_ref, k, p).astype(jnp.int32) - own_base
        for k in range(2)
        for p in range(PAIRS_IN)
    }
    ids = jnp.where(lane == 6, leaving_stiff, 0.0)
    for k in range(2):
        for p in range(PAIRS_IN):
            ids = jnp.where(lane == k * PAIRS_IN + p, targets[k, p], ids)
    id_out[...] = ids

    def send(source, target, send_sem, recv_sem, device):
        copy = pltpu.make_async_remote_copy(
            src_ref=source,
            dst_ref=target,
            send_sem=send_sem,
            recv_sem=recv_sem,
            device_id=device,
            device_id_type=MESH,
        )
        copy.start()
        return copy

    sent = []
    def targets_of(k):
        masks = []
        for l, (pair, _) in enumerate(links):
            target = jnp.sum(
                jnp.where(lane == k * PAIRS_IN + pair, id_in[l], 0.0), axis=1, keepdims=True
            )
            masks.append(row_of == target.astype(jnp.int32) - own_base)
        masks.append(row_of == targets[k, 1].astype(jnp.int32) - own_base)
        return [mask.astype(jnp.float32) for mask in masks]

    fourth = fourth_ref[...]
    operand_row = lax.broadcasted_iota(jnp.int32, (8, columns), 0)

    def product_of(fields, k, p):
        mask = row_wide == sources[k, p]
        stacked = jnp.zeros((8, columns), jnp.float32)
        for j, field in enumerate(fields):
            picked = jnp.sum(jnp.where(mask, field, 0.0), axis=0, keepdims=True)
            stacked = jnp.where(lax.rem(operand_row, 4) == j, picked, stacked)
        high = stacked.astype(jnp.bfloat16).astype(jnp.float32)
        operand = jnp.where(operand_row < 4, high, stacked - high).astype(jnp.bfloat16)
        product = dot_nt(operand, block_buf[k, p])
        product = product[0:4] + product[4:8]
        return product[0:1] if len(fields) == 1 else product

    def ends_of(exchange):
        if exchange >= ITERS:
            return wide_out.at[exchange - ITERS], wide_in.at[exchange - ITERS]
        return near_out.at[exchange], near_in.at[exchange]

    def launch(exchange, p):
        source, target = ends_of(exchange)
        copies = {
            l: send(
                source.at[pair],
                target.at[l],
                near_send.at[exchange, l],
                near_recv.at[exchange, l],
                device,
            )
            for l, (pair, device) in enumerate(links)
            if pair == p
        }
        sent.extend(copies.values())
        return copies

    def dispatch(fields, k, exchange):
        copies = {}
        for p in (0, 2, 1):
            own = product_of(fields, k, p)
            ends_of(exchange)[0][p] = own
            copies.update(launch(exchange, p))
        return own, copies

    def bend(fields, bending):
        halves = [f[:, i * points : (i + 1) * points] for f in fields for i in range(2)]
        curved = jnp.dot(
            jnp.concatenate(halves, axis=0),
            fourth,
            preferred_element_type=jnp.float32,
            precision=lax.Precision.HIGHEST,
        )
        images = []
        for j, field in enumerate(fields):
            x_part = curved[2 * j * rows : (2 * j + 1) * rows]
            y_part = curved[(2 * j + 1) * rows : (2 * j + 2) * rows]
            images.append(field + bending * jnp.concatenate([x_part, y_part], axis=1))
        return images

    def receive(images, own, copies, exchange, masks):
        wide = exchange >= ITERS
        images = [image + masks[LINKS] * own[j : j + 1] for j, image in enumerate(images)]
        for l in sorted(copies):
            copies[l].wait_recv()
            arrived = wide_in[exchange - ITERS, l] if wide else near_in[exchange, l]
            images = [
                image + masks[l] * arrived[j : j + 1] for j, image in enumerate(images)
            ]
        return [image * (1.0 / GAMMA) for image in images]

    def folded(product):
        wide = total_of(product[:, i * 128 : (i + 1) * 128] for i in range(columns // 128))
        return jnp.sum(wide, axis=0, keepdims=True)

    gram_pairs = [(i, j) for i in range(ITERS + 1) for j in range(i, ITERS + 1)]

    diagonal = lax.broadcasted_iota(jnp.int32, (16, 128), 0) == lax.broadcasted_iota(
        jnp.int32, (16, 128), 1
    )

    def gram_sums(basis):
        for n, (i, j) in enumerate(gram_pairs):
            gram_buf[n : n + 1, :] = folded(basis[i] * basis[j])
        sums = jnp.sum(gram_buf[...], axis=1, keepdims=True)
        return jnp.sum(jnp.where(diagonal, sums, 0.0), axis=0, keepdims=True)

    order = [1, 0]
    inboxes = (sum_in_0, sum_in_1)

    def stage_start(values, which, t):
        stage, inbox = stages[t], inboxes[t]
        first = sum(len(s) for s in stages[:t])
        sum_out[which, t] = values
        copies = [
            send(
                sum_out.at[which, t],
                inbox.at[which, i],
                sum_send.at[which, first + i],
                sum_recv.at[which, first + i],
                device,
            )
            for i, device in enumerate(stage)
        ]
        sent.extend(copies)
        return copies

    def stage_end(values, copies, which, t):
        for i, copy in enumerate(copies):
            copy.wait_recv()
            values = values + inboxes[t][which, i]
        return values

    def weights_of(values):
        spread = jnp.sum(jnp.where(diagonal, values, 0.0), axis=1, keepdims=True)
        scalar_buf[...] = jnp.broadcast_to(spread, scalar_buf.shape)
        weights = krylov_weights(
            {pair: scalar_buf[n : n + 1, :] for n, pair in enumerate(gram_pairs)}
        )
        return [jnp.broadcast_to(weight[:, 0:1], (rows, columns)) for weight in weights]

    def cross(field, j):
        row_out[j] = jnp.sum(jnp.where(row_wide == slot, field, 0.0), axis=0, keepdims=True)
        copy = send(row_out.at[j], row_in.at[j], row_send.at[j], row_recv.at[j], links[3][1])
        sent.append(copy)
        return copy

    gram_buf[...] = jnp.zeros_like(gram_buf)
    start = pos_ref[...]
    loads[0].wait()
    for p in (0, 2, 1):
        own = product_of([start], 0, p)
        near_out[0, p] = own
    images = bend([start], stiff)

    pl.semaphore_wait(barrier, len(greeted))
    copies = {l: copy for p in (0, 2, 1) for l, copy in launch(0, p).items()}
    id_copies = [
        send(id_out, id_in.at[l], id_send.at[l], id_recv.at[l], device)
        for l, (_, device) in enumerate(links)
    ]
    sent += id_copies
    if reach:
        tell(0)
    for device in columns_y:
        pl.semaphore_signal(ready_sem.at[3], inc=1, device_id=device, device_id_type=MESH)
    crossings = [cross(start, 0)]
    loads[1].wait()
    for copy in id_copies:
        copy.wait_recv()
    masks = targets_of(0)
    later_masks = targets_of(1)
    new_stiff = jnp.sum(jnp.where(lane == 6, id_in[3], 0.0), axis=1, keepdims=True)
    moved_stiff = jnp.where(row_of == slot, new_stiff, stiff)

    basis = [start] + receive(images, own, copies, 0, masks)
    for j in range(1, ITERS):
        own, copies = dispatch([basis[j]], 0, j)
        crossings.append(cross(basis[j], j))
        if j - 1 < len(reach):
            hear(j - 1)
            if j < len(reach):
                tell(j)
        images = bend([basis[j]], stiff)
        basis += receive(images, own, copies, j, masks)

    if columns_y:
        pl.semaphore_wait(ready_sem.at[3], len(columns_y))
    for n in range(ITERS - 1, len(reach)):
        hear(n)
        if n + 1 < len(reach):
            tell(n + 1)
    level = []
    for j in range(ITERS):
        crossings[j].wait_recv()
        level.append(jnp.where(row_wide == slot, row_in[j], basis[j]))
    levels = [level]
    flying = None
    for j in range(ITERS):
        exchange = ITERS + j
        own, copies = dispatch(levels[j], 1, exchange)
        if j == 0:
            values = gram_sums(basis)
        elif j <= len(order):
            values = stage_end(values, flying, 0, order[j - 1])
        if j < len(order):
            flying = stage_start(values, 0, order[j])
        elif j == len(order):
            weights = weights_of(values)
        images = bend(levels[j], moved_stiff)
        levels.append(receive(images, own, copies, exchange, later_masks))
    second = [total_of(w * part for w, part in zip(weights, parts)) for parts in levels]
    after_ref[...] = second[0]
    values = gram_sums(second)
    done = list(sent)
    for t in order:
        flying = stage_start(values, 1, t)
        if t == order[0]:
            for copy in done:
                copy.wait_send()
        values = stage_end(values, flying, 1, t)
    weights = weights_of(values)
    final_ref[...] = total_of(w * part for w, part in zip(weights, second))
    for copy in sent[len(done) :]:
        copy.wait_send()


def local(sizes, table, positions, stiffness, blocks, pair_src, pair_tgt, cross_slots):
    rows, columns = positions.shape
    ny, nz, nx, nc, nr = sizes
    peers = (ny * nx * nc * nr - 1, nz - 1)
    vmem = pl.BlockSpec(memory_space=pltpu.VMEM)
    f32 = jnp.float32
    dma = pltpu.SemaphoreType.DMA
    after_crossing, final_positions = pl.pallas_call(
        functools.partial(kernel, sizes),
        out_shape=(pltpu.VMEM((rows, columns), f32),) * 2,
        in_specs=[pl.BlockSpec(memory_space=pltpu.HBM)] * 7,
        out_specs=(vmem, vmem),
        scratch_shapes=[
            pltpu.VMEM(pair_src.shape, jnp.int32),
            pltpu.VMEM(pair_tgt.shape, jnp.int32),
            pltpu.VMEM(cross_slots.shape, jnp.int32),
            pltpu.VMEM((rows, columns), f32),
            pltpu.VMEM((1, rows), f32),
            pltpu.VMEM(table.shape, f32),
            pltpu.VMEM(blocks.shape, blocks.dtype),
            pltpu.VMEM((1, 128), f32),
            pltpu.VMEM((LINKS, 1, 128), f32),
            pltpu.VMEM((ITERS, PAIRS_IN, 1, columns), f32),
            pltpu.VMEM((ITERS, LINKS, 1, columns), f32),
            pltpu.VMEM((ITERS, PAIRS_IN, 4, columns), f32),
            pltpu.VMEM((ITERS, LINKS, 4, columns), f32),
            pltpu.VMEM((ITERS, 1, columns), f32),
            pltpu.VMEM((ITERS, 1, columns), f32),
            pltpu.VMEM((16, 128), f32),
            pltpu.VMEM((16, 128), f32),
            pltpu.VMEM((2, 2, 1, 128), f32),
            pltpu.VMEM((2, max(peers[0], 1), 1, 128), f32),
            pltpu.VMEM((2, max(peers[1], 1), 1, 128), f32),
            dma((6,)),
            dma((2,)),
            pltpu.SemaphoreType.REGULAR((4,)),
            dma((LINKS,)),
            dma((LINKS,)),
            dma((2 * ITERS, LINKS)),
            dma((2 * ITERS, LINKS)),
            dma((ITERS,)),
            dma((ITERS,)),
            dma((2, sum(peers))),
            dma((2, sum(peers))),
        ],
        compiler_params=pltpu.CompilerParams(collective_id=0, has_side_effects=True),
    )(
        pair_src,
        pair_tgt,
        cross_slots,
        positions,
        stiffness.reshape(1, rows),
        jnp.asarray(table),
        blocks,
    )
    return after_crossing, final_positions


def program(split):
    sizes = tuple(split.shape[name] for name in SECTOR_RADIAL)
    placed = (
        P(SECTOR_RADIAL, None),
        P(SECTOR_RADIAL),
        P(None, SECTOR_RADIAL, None, None),
        P(None, SECTOR_RADIAL),
        P(None, SECTOR_RADIAL),
        P(SECTOR_RADIAL, None),
    )
    return jax.shard_map(
        functools.partial(local, sizes, bending_table(256)),
        mesh=split,
        in_specs=placed,
        out_specs=(P(SECTOR_RADIAL, None), P(SECTOR_RADIAL, None)),
        check_vma=False,
    )


def solution(mesh):
    split = Mesh(mesh.devices.reshape(4, 16, 2, 2, mesh.shape["radial"]), SECTOR_RADIAL)
    return program(split)
```
